32 devices in a mesh: dp: 16 (over z, y, core), mp: 2 (over x).
Axes of the slice: x: 2, y: 2, z: 4, core: 2. Of those that a mesh axis runs over, the one named last changes fastest.
Arguments:
- image_tokens: bfloat16 [48, 256, 1536], P('dp', 'mp'), may hold values from -6 to 6
- text_tokens: bfloat16 [48, 128, 1536], P('dp', 'mp'), may hold values from -6 to 6
- condition: bfloat16 [48, 1536], P('dp', 'mp'), may hold values from -6 to 6
- live_table: int32 [16, 3], P('dp'), may hold values from 0 to 1, as said below
- ada_weight: float32 [2, 1536, 9216], P(None, ('mp', 'dp')), may hold values from -0.15625 to 0.15625
- ada_bias: float32 [2, 9216], P(None, 'dp'), may hold values from -3 to 3
- qkv_weight: float32 [2, 3, 1536, 1536], P(None, None, 'dp', 'mp'), may hold values from -0.15625 to 0.15625
- qv_bias: float32 [2, 2, 1536], P(None, None, ('mp', 'dp')), may hold values from -3 to 3
- proj_weight: float32 [2, 1536, 1536], P(None, 'mp', 'dp'), may hold values from -1.25 to 1.25
- proj_bias: float32 [2, 1536], P(None, 'dp'), may hold values from -3 to 3
- fc1_weight: float32 [2, 1536, 6144], P(None, 'dp', 'mp'), may hold values from -0.15625 to 0.15625
- fc1_bias: float32 [2, 6144], P(None, ('mp', 'dp')), may hold values from -3 to 3
- fc2_weight: float32 [2, 6144, 1536], P(None, 'mp', 'dp'), may hold values from -0.078125 to 0.078125
- fc2_bias: float32 [2, 1536], P(None, 'dp'), may hold values from -3 to 3
- image_cotangent: bfloat16 [48, 256, 1536], P('dp', 'mp'), may hold values from -6 to 6
- text_cotangent: bfloat16 [48, 128, 1536], P('dp', 'mp'), may hold values from -6 to 6
Outputs:
- image_out: bfloat16 [48, 256, 1536], P('dp', 'mp')
- text_out: bfloat16 [48, 128, 1536], P('dp', 'mp')
- ada_weight_grad: float32 [2, 1536, 9216], P(None, ('mp', 'dp'))
- ada_bias_grad: float32 [2, 9216], P(None, 'dp')
- qkv_weight_grad: float32 [2, 3, 1536, 1536], P(None, None, 'dp', 'mp')
- qv_bias_grad: float32 [2, 2, 1536], P(None, None, ('mp', 'dp'))
- proj_weight_grad: float32 [2, 1536, 1536], P(None, 'mp', 'dp')
- proj_bias_grad: float32 [2, 1536], P(None, 'dp')
- fc1_weight_grad: float32 [2, 1536, 6144], P(None, 'dp', 'mp')
- fc1_bias_grad: float32 [2, 6144], P(None, ('mp', 'dp'))
- fc2_weight_grad: float32 [2, 6144, 1536], P(None, 'mp', 'dp')
- fc2_bias_grad: float32 [2, 1536], P(None, 'dp')
- image_grad: float32 [48, 256, 1536], P('dp', 'mp')
- text_grad: float32 [48, 128, 1536], P('dp', 'mp')
- condition_grad: float32 [48, 1536], P('dp', 'mp')
The draws below stay inside these ranges and needn't reach their ends.
Inputs may be any that keep to these rules, and one draw needn't show every extreme that they name: `live_table`: every row has a live entry, and some row has all 3 entries live.
All inputs are finite; a program needn't handle non-finite values.
Results may differ from the reference program's by a relative error of at most 0.02.
The reference program's roundings to bfloat16 on the way count: a program that leaves them out, or rounds other values in their place, can miss the bound.
Values may be sent and summed in bfloat16 or wider, within the bound.
No kernel may reach another device: no remote copies, remote signals or barrier semaphores. Data moves between devices by JAX's collectives and lax.ppermute only.
A program may use at most 960 MiB of HBM per device.

```python
import jax
import jax.numpy as jnp
from jax import lax

D = 1536
HEADS = 24
HEAD_DIM = 64
FF = 6144
IMG = 256
TXT = 128
MB = 3
SEQS = 48
N_DP = 16


def draw_live_table(key, part):
    key_live, key_column, key_row = jax.random.split(key, 3)
    live_rows = (jax.random.randint(key_live, (N_DP, MB), 0, 4) > 0).astype(jnp.int32)
    column = jax.random.randint(key_column, (N_DP,), 0, MB)
    forced = (jnp.arange(MB)[None, :] == column[:, None]).astype(jnp.int32)
    live_rows = jnp.maximum(live_rows, forced)
    chosen = jax.random.randint(key_row, (), 0, N_DP)
    full_row = (jnp.arange(N_DP)[:, None] == chosen).astype(jnp.int32)
    return jnp.maximum(live_rows, full_row)


def level_of(stream_key, dims, cuts, low, top_value):
    level = 1.0
    for axis_at, blocks in cuts:
        draws = jax.random.uniform(jax.random.fold_in(jax.random.fold_in(stream_key, 6), axis_at), (blocks,), jnp.float32, low / len(cuts), top_value / len(cuts))
        level = level * jnp.repeat(jnp.exp(draws), dims[axis_at] // blocks).reshape((-1,) + (1,) * (len(dims) - 1 - axis_at))
    return level


def scatter_about(stream_key, dims, width, bound, cuts=(), kind=jnp.bfloat16):
    values = jax.random.normal(stream_key, dims, jnp.float32) * width
    if len(cuts) > 0:
        values = level_of(stream_key, dims, cuts, -0.22, 0.18) * values
    return jnp.clip(values, min=-bound, max=bound).astype(kind)


def setup_inputs(seed: int = 0) -> dict:
    seeds = jax.random.split(jax.random.key(seed), 17)
    image_tokens = scatter_about(seeds[0], (SEQS, IMG, D), 1.0, 6.0, ((0, 16), (1, 2)))
    text_tokens = scatter_about(seeds[1], (SEQS, TXT, D), 1.0, 6.0, ((0, 16), (1, 2)))
    condition = scatter_about(seeds[2], (SEQS, D), 1.0, 6.0, ((0, 16), (1, 2)))
    live_table = draw_live_table(jax.random.fold_in(seeds[16], 71), 0)
    ada_weight = scatter_about(seeds[4], (2, D, 6 * D), D ** -0.5, 0.15625, ((1, 32),), jnp.float32)
    ada_bias = scatter_about(seeds[5], (2, 6 * D), 0.5, 3.0, ((1, 16),), jnp.float32)
    qkv_weight = scatter_about(seeds[6], (2, 3, D, D), D ** -0.5, 0.15625, ((2, 16), (3, 2)), jnp.float32)
    qv_bias = scatter_about(seeds[7], (2, 2, D), 0.5, 3.0, ((2, 32),), jnp.float32)
    proj_weight = scatter_about(seeds[8], (2, D, D), (D // 64) ** -0.5, 1.25, ((1, 2), (2, 16)), jnp.float32)
    proj_bias = scatter_about(seeds[9], (2, D), 0.5, 3.0, ((1, 16),), jnp.float32)
    fc1_weight = scatter_about(seeds[10], (2, D, FF), D ** -0.5, 0.15625, ((1, 16), (2, 2)), jnp.float32)
    fc1_bias = scatter_about(seeds[11], (2, FF), 0.5, 3.0, ((1, 32),), jnp.float32)
    fc2_weight = scatter_about(seeds[12], (2, FF, D), FF ** -0.5, 0.078125, ((1, 2), (2, 16)), jnp.float32)
    fc2_bias = scatter_about(seeds[13], (2, D), 0.5, 3.0, ((1, 16),), jnp.float32)
    image_cotangent = scatter_about(seeds[14], (SEQS, IMG, D), 1.0, 6.0, ((0, 16), (1, 2)))
    text_cotangent = scatter_about(seeds[15], (SEQS, TXT, D), 1.0, 6.0, ((0, 16), (1, 2)))
    return dict(image_tokens=image_tokens, text_tokens=text_tokens, condition=condition, live_table=live_table, ada_weight=ada_weight, ada_bias=ada_bias, qkv_weight=qkv_weight, qv_bias=qv_bias, proj_weight=proj_weight, proj_bias=proj_bias, fc1_weight=fc1_weight, fc1_bias=fc1_bias, fc2_weight=fc2_weight, fc2_bias=fc2_bias, image_cotangent=image_cotangent, text_cotangent=text_cotangent)


EPSILON = 1e-06

@jax.custom_vjp
def low(v):
    return lax.optimization_barrier(v.astype(jnp.bfloat16)).astype(jnp.float32)

@jax.custom_vjp
def low_back(v):
    return v

def low_keep(v):
    return (low(v), None)

def low_pass(kept, grad):
    return (grad,)

def back_keep(v):
    return (v, None)

def back_low(kept, grad):
    return (low(grad),)
low.defvjp(low_keep, low_pass)
low_back.defvjp(back_keep, back_low)

def matmul(left, right):
    return jnp.dot(left, right, precision=lax.Precision.HIGHEST, preferred_element_type=jnp.float32)

def layer_norm(values):
    center = values - lax.optimization_barrier(jnp.mean(values, axis=-1, keepdims=True))
    return center * lax.rsqrt(lax.optimization_barrier(jnp.mean(center * center, axis=-1, keepdims=True)) + EPSILON)

def head_attention(operands):
    query_head, key_head, value_head = operands
    scores = low_back(matmul(query_head, key_head.T) * HEAD_DIM ** (-0.5))
    weights = low(jax.nn.softmax(scores, axis=-1))
    return matmul(weights, value_head)

def sequence_forward(masters, image_rows, text_rows, cond_row):
    rounded = [low(master) for master in masters]
    ada_weights, ada_biases, qkv_weights, qv_biases, proj_weights = rounded[0:5]
    proj_biases, up_weights, up_biases, down_weights, down_biases = rounded[5:10]
    silu_cond = low(jax.nn.silu(cond_row))
    streams = (image_rows, text_rows)
    groups = []
    columns = [[], [], []]
    for stream in range(2):
        modulation = matmul(silu_cond[None, :], ada_weights[stream])[0] + ada_biases[stream]
        pieces = jnp.split(modulation, 6)
        groups.append(pieces)
        joint_in = low(layer_norm(streams[stream]) * (1.0 + pieces[1]) + pieces[0])
        for select in range(3):
            product = matmul(joint_in, qkv_weights[stream, select])
            if select == 0:
                product = product + qv_biases[stream, 0]
            if select == 2:
                product = product + qv_biases[stream, 1]
            columns[select].append(low(low_back(product)))
    heads_list = []
    for select in range(3):
        joined = jnp.concatenate([columns[select][1], columns[select][0]], axis=0)
        heads_list.append(joined.reshape(joined.shape[0], HEADS, HEAD_DIM).transpose(1, 0, 2))
    attended = lax.map(jax.checkpoint(head_attention), tuple(heads_list))
    total_len = attended.shape[1]
    attended = low(low_back(attended.transpose(1, 0, 2).reshape(total_len, HEADS * HEAD_DIM)))
    text_len = text_rows.shape[0]
    mixed_rows = (attended[text_len:], attended[:text_len])
    outputs = []
    for stream in range(2):
        pieces = groups[stream]
        branch = low_back(matmul(mixed_rows[stream], proj_weights[stream])) + proj_biases[stream]
        residual = streams[stream] + pieces[2] * branch
        mlp_in = low(layer_norm(residual) * (1.0 + pieces[4]) + pieces[3])
        pre_active = low_back(matmul(mlp_in, up_weights[stream]) + up_biases[stream])
        activated = low(jax.nn.gelu(pre_active, approximate=True))
        second = low_back(matmul(activated, down_weights[stream])) + down_biases[stream]
        outputs.append(residual + pieces[5] * second)
    return (outputs[0], outputs[1])

def reference(image_tokens, text_tokens, condition, live_table, ada_weight, ada_bias, qkv_weight, qv_bias, proj_weight, proj_bias, fc1_weight, fc1_bias, fc2_weight, fc2_bias, image_cotangent, text_cotangent):
    masters = (ada_weight, ada_bias, qkv_weight, qv_bias, proj_weight, proj_bias, fc1_weight, fc1_bias, fc2_weight, fc2_bias)
    flags = live_table.reshape(-1).astype(jnp.float32)

    def one_sequence(totals, inputs):
        image_rows, text_rows, cond_row, flag_value, image_back, text_back = inputs
        outputs, pullback = jax.vjp(sequence_forward, masters, image_rows.astype(jnp.float32), text_rows.astype(jnp.float32), cond_row.astype(jnp.float32))
        grads = pullback((image_back.astype(jnp.float32) * flag_value, text_back.astype(jnp.float32) * flag_value))
        totals = jax.tree.map(jnp.add, totals, tuple(grads[0]))
        emitted = ((outputs[0] * flag_value).astype(jnp.bfloat16), (outputs[1] * flag_value).astype(jnp.bfloat16), grads[1], grads[2], grads[3])
        return (totals, emitted)
    initial = tuple((jnp.zeros(master.shape, jnp.float32) for master in masters))
    totals, emitted = lax.scan(one_sequence, initial, (image_tokens, text_tokens, condition, flags, image_cotangent, text_cotangent))
    return (emitted[0], emitted[1], totals[0], totals[1], totals[2], totals[3], totals[4], totals[5], totals[6], totals[7], totals[8], totals[9], emitted[2], emitted[3], emitted[4])
```

```python
import functools

import jax
import jax.numpy as jnp
from jax import lax
from jax.experimental import pallas as pl
from jax.experimental.pallas import tpu as pltpu
from jax.sharding import PartitionSpec as P

HEAD_DIM = 64
EPSILON = 1e-06
F32 = jnp.float32
BF16 = jnp.bfloat16


def layer_norm(values):
    center = values - jnp.mean(values, axis=-1, keepdims=True)
    inverse = lax.rsqrt(jnp.mean(center * center, axis=-1, keepdims=True) + EPSILON)
    return (center * inverse, inverse)


def norm_back(normed, inverse, upstream):
    mean_up = jnp.mean(upstream, axis=-1, keepdims=True)
    mean_cross = jnp.mean(upstream * normed, axis=-1, keepdims=True)
    return inverse * (upstream - mean_up - normed * mean_cross)


def gelu_tanh(values):
    return jax.nn.gelu(values, approximate=True)


def dot(left, right, dims):
    return lax.dot_general(left, right, (dims, ((), ())), preferred_element_type=F32)


NN = ((1,), (0,))
NT = ((1,), (1,))
TN = ((0,), (0,))


def join_rows(text_ref, image_ref):
    width = text_ref.shape[-1]
    return jnp.concatenate(
        [text_ref[...].reshape(-1, width), image_ref[...].reshape(-1, width)], axis=0
    )


def attention_kernel(qi, ki, vi, qt, kt, vt, oi, ot):
    query, key, value = join_rows(qt, qi), join_rows(kt, ki), join_rows(vt, vi)
    width = query.shape[1]
    head_of = lax.broadcasted_iota(jnp.int32, query.shape, 1) // HEAD_DIM
    out = jnp.zeros(query.shape, F32)
    for head in range(width // HEAD_DIM):
        inside = head_of == head
        scores = dot(jnp.where(inside, query, jnp.zeros_like(query)), key, NT) * HEAD_DIM**-0.5
        raised = jnp.exp(scores - jnp.max(scores, axis=1, keepdims=True))
        probs = raised * (1.0 / jnp.sum(raised, axis=1, keepdims=True))
        out = jnp.where(inside, dot(probs.astype(BF16), value, NN), out)
    text_rows = ot.shape[0] * ot.shape[1]
    ot[...] = out[:text_rows].astype(BF16).reshape(ot.shape)
    oi[...] = out[text_rows:].astype(BF16).reshape(oi.shape)


def attention_back_kernel(qi, ki, vi, gi, qt, kt, vt, gt, di, dt):
    query, key, value, grad = (
        join_rows(qt, qi),
        join_rows(kt, ki),
        join_rows(vt, vi),
        join_rows(gt, gi),
    )
    width = query.shape[1]
    head_of = lax.broadcasted_iota(jnp.int32, query.shape, 1) // HEAD_DIM
    blank = jnp.zeros_like(query)
    dq, dk, dv = (jnp.zeros(query.shape, F32) for _ in range(3))
    scale = HEAD_DIM**-0.5
    for head in range(width // HEAD_DIM):
        inside = head_of == head
        scores = dot(jnp.where(inside, key, blank), query, NT) * scale
        raised = jnp.exp(scores - jnp.max(scores, axis=0, keepdims=True))
        probs = raised * (1.0 / jnp.sum(raised, axis=0, keepdims=True))
        grad_probs = dot(jnp.where(inside, value, blank), grad, NT)
        delta = jnp.sum(probs * grad_probs, axis=0, keepdims=True)
        grad_scores = (probs * (grad_probs - delta)).astype(BF16)
        dv = jnp.where(inside, dot(probs.astype(BF16), grad, NN), dv)
        dk = jnp.where(inside, dot(grad_scores, query, NN) * scale, dk)
        dq = jnp.where(inside, dot(grad_scores, key, TN) * scale, dq)
    text_rows = dt.shape[1] * dt.shape[2]
    for place, value_now in enumerate((dq, dk, dv)):
        low = value_now.astype(BF16)
        dt[place] = low[:text_rows].reshape(dt.shape[1:])
        di[place] = low[text_rows:].reshape(di.shape[1:])


def head_block(width):
    return 128 if width % 128 == 0 else width


def picked(array, place, lanes, first=0):
    groups, rows = array.shape[1], array.shape[3]
    return pl.BlockSpec(
        (None, groups, None, rows, lanes), lambda seq, block: (place, 0, seq + first, 0, block)
    )


def plain(array, lanes, first=0):
    groups, rows = array.shape[0], array.shape[2]
    return pl.BlockSpec(
        (groups, None, rows, lanes), lambda seq, block: (0, seq + first, 0, block)
    )


def attention_forward(image, text):
    seqs, width = image.shape[2], image.shape[4]
    lanes = head_block(width)
    shapes = [jax.ShapeDtypeStruct(a.shape[1:], BF16) for a in (image, text)]
    return pl.pallas_call(
        attention_kernel,
        grid=(seqs, width // lanes),
        in_specs=[picked(a, place, lanes) for a in (image, text) for place in range(3)],
        out_specs=[plain(s, lanes) for s in shapes],
        out_shape=shapes,
        compiler_params=pltpu.CompilerParams(
            dimension_semantics=("parallel", "parallel"), vmem_limit_bytes=48 * 2**20
        ),
        name="attention_forward",
    )(image, image, image, text, text, text)


def attention_backward(image, text, image_grad, text_grad, first):
    width = image.shape[4]
    lanes = head_block(width)

    def whole(shape):
        return pl.BlockSpec(
            (3, shape[1], None, shape[3], lanes), lambda seq, block: (0, 0, seq, 0, block)
        )

    specs = []
    for array, grad in ((image, image_grad), (text, text_grad)):
        specs += [picked(array, place, lanes, first) for place in range(3)]
        specs.append(plain(grad, lanes, first))
    shapes = [a.shape[:2] + (1,) + a.shape[3:] for a in (image, text)]
    return pl.pallas_call(
        attention_back_kernel,
        grid=(1, width // lanes),
        in_specs=specs,
        out_specs=[whole(shape) for shape in shapes],
        out_shape=[jax.ShapeDtypeStruct(shape, BF16) for shape in shapes],
        compiler_params=pltpu.CompilerParams(
            dimension_semantics=("parallel", "parallel"), vmem_limit_bytes=48 * 2**20
        ),
        name="attention_backward",
    )(image, image, image, image_grad, text, text, text, text_grad)


def ring_of(chips):
    wide = 1
    while (2 * wide) ** 2 <= chips:
        wide *= 2
    long = chips // wide
    order = [row * wide for row in range(long)]
    for turn, row in enumerate(reversed(range(long))):
        across = list(range(1, wide))
        order += [row * wide + col for col in (across if turn % 2 == 0 else across[::-1])]
    return order


class Ring:
    def __init__(self, stream, dp, kind=BF16):
        self.kind, self.dp = kind, dp
        self.chips = dp // 2
        order = ring_of(self.chips)
        me = lax.axis_index("dp")
        chip, self.core = me // 2, me % 2
        way = 1 if stream == 0 else -1
        self.hop = [
            (2 * order[i] + c, 2 * order[(i + way) % self.chips] + c)
            for i in range(self.chips)
            for c in range(2)
        ]
        self.targets = []
        for step in range(self.chips):
            at = jnp.int32(0)
            for spot, here in enumerate(order):
                at = at + jnp.where(chip == here, order[(spot - way * (1 + step)) % self.chips], 0)
            self.targets.append(at)
        self.views, self.flying = [], []
        self.step = 0
        self.result = None

    def give(self, grad):
        view = grad.astype(self.kind).reshape((self.chips, 2, -1, grad.shape[-1]))
        gift = lax.dynamic_index_in_dim(view, 1 - self.core, 1, False)
        self.views.append(view)
        self.flying.append(lax.ppermute(gift, "dp", [(i, i ^ 1) for i in range(self.dp)]))

    def block(self):
        at = self.targets[self.step]
        parts = []
        for view, got in zip(self.views, self.got):
            start = (at, self.core, 0, 0)
            kept = lax.dynamic_slice(view, start, (1, 1) + view.shape[2:])[0, 0]
            came = lax.dynamic_index_in_dim(got, at, 0, False)
            parts.append(kept.astype(F32) + came.astype(F32))
        return jnp.concatenate(parts, axis=1)

    def advance(self):
        if self.step == 0:
            self.got = self.flying
            total = self.block()
        else:
            total = self.flying[0].astype(F32) + self.block()
        if self.step == self.chips - 1:
            self.result = total
            self.flying = []
        else:
            self.flying = [lax.ppermute(total.astype(self.kind), "dp", self.hop)]
        self.step += 1

    def finish(self):
        while self.result is None:
            self.advance()
        return self.result


def beat(value, *groups):
    for number, group in enumerate(groups):
        if group[0].result is not None:
            continue
        value, flights = lax.optimization_barrier((value, [ring.flying for ring in group]))
        for ring, flight in zip(group, flights):
            ring.flying = flight
            ring.advance()
        if group[0].result is None:
            return value
        if number + 1 == len(groups) or not groups[number + 1][0].flying:
            return value
    return value


def tie(*values):
    return lax.optimization_barrier(values)


def body(
    mp,
    dp,
    image_tokens,
    text_tokens,
    condition,
    live_table,
    ada_weight,
    ada_bias,
    qkv_weight,
    qv_bias,
    proj_weight,
    proj_bias,
    fc1_weight,
    fc1_bias,
    fc2_weight,
    fc2_bias,
    image_cotangent,
    text_cotangent,
):
    seqs, width = image_tokens.shape[0], image_tokens.shape[2]
    my_dp = lax.axis_index("dp")
    swap = [(0, 1), (1, 0)]

    def share(rows):
        if mp == 2:
            return jnp.stack([rows, lax.ppermute(rows, "mp", swap)])
        return lax.all_gather(rows, "mp", axis=0, tiled=False)

    def collect(parts):
        if mp == 2:
            return parts[0] + lax.ppermute(parts[1].astype(BF16), "mp", swap).astype(F32)
        low = parts.astype(BF16)
        return lax.psum_scatter(low, "mp", scatter_dimension=0, tiled=False).astype(F32)

    def sum_mp(values):
        if mp == 2:
            return values + lax.ppermute(values, "mp", swap)
        return lax.psum(values, "mp")

    def flat(array):
        return array.reshape(-1, array.shape[-1])

    def gather_small(rows):
        reach = 1
        while reach < dp:
            other = lax.ppermute(rows, "dp", [(i, i ^ reach) for i in range(dp)])
            low_half = (my_dp & reach) == 0
            rows = jnp.concatenate(
                [jnp.where(low_half, rows, other), jnp.where(low_half, other, rows)], axis=0
            )
            reach *= 2
        return rows

    def gather_vector(vector):
        vector = jnp.pad(vector, (0, -vector.size % 2048)).reshape(1, -1, 128)
        return lax.all_gather(vector, "dp", axis=0, tiled=True).reshape(dp, -1)

    small = [condition, ada_bias, qv_bias, proj_bias, fc1_bias, fc2_bias]
    sizes = [a.size for a in small]
    packed = jnp.concatenate([a.astype(BF16).reshape(-1) for a in small])
    packed = jnp.pad(packed, (0, -packed.size % 2048)).reshape(1, -1, 128)
    packed = gather_small(packed).reshape(dp, -1)
    pieces, at = [], 0
    for array, size in zip(small, sizes):
        pieces.append(packed[:, at : at + size].reshape((dp,) + array.shape))
        at += size
    cond_all = pieces[0].reshape(dp * seqs, -1)
    ada_biases, proj_biases, up_biases, down_biases = (
        jnp.moveaxis(pieces[i], 0, 1).reshape(2, -1).astype(F32) for i in (1, 3, 4, 5)
    )
    qv_biases = jnp.moveaxis(pieces[2], 0, 2).reshape(2, 2, -1).astype(F32)

    attention_low = [qkv_weight.astype(BF16), jnp.swapaxes(proj_weight.astype(BF16), 1, 2)[:, None]]
    attention_full = lax.all_gather(
        jnp.concatenate(attention_low, axis=1), "dp", axis=2, tiled=True
    )
    up_full = lax.all_gather(fc1_weight.astype(BF16), "dp", axis=1, tiled=True)
    down_full = lax.all_gather(
        jnp.swapaxes(fc2_weight.astype(BF16), 1, 2), "dp", axis=1, tiled=True
    )

    ada_low = ada_weight.astype(BF16)
    ada_rows = ada_low.shape[1]
    silu_all = jax.nn.silu(cond_all.astype(F32)).astype(BF16)
    silu_mine = lax.dynamic_slice_in_dim(silu_all, my_dp * ada_rows, ada_rows, axis=1)
    mod_rings = []
    for s in range(2):
        mod_rings.append(Ring(s, dp, F32))
        mod_rings[s].give(dot(silu_mine, ada_low[s], NN).reshape(-1, 128))
    modulation = jnp.stack([ring.finish().reshape(seqs, -1) for ring in mod_rings], axis=1)
    modulation = sum_mp(modulation) + ada_biases
    modulation = modulation.reshape(seqs, 2, 6, 1, width)

    def mod(stream, which):
        return modulation[:, stream, which]

    live = live_table[0].astype(F32)[:, None, None]
    tokens = [image_tokens.astype(F32), text_tokens.astype(F32)]
    cotangents = [image_cotangent.astype(F32) * live, text_cotangent.astype(F32) * live]

    first_norm, first_inverse, joint_in = [], [], []
    for s in range(2):
        normed, inverse = layer_norm(tokens[s])
        first_norm.append(normed)
        first_inverse.append(inverse)
        joint_in.append(share((normed * (1.0 + mod(s, 1)) + mod(s, 0)).astype(BF16)))

    branch_grad = [cotangents[s] * mod(s, 5) for s in range(2)]
    branch_low, joint_in = tie([b.astype(BF16) for b in branch_grad], joint_in)
    down_up = [share(branch_low[s]) for s in range(2)]

    qkv = []
    for s in range(2):
        rows = flat(joint_in[s])
        products = []
        for t in range(3):
            product = dot(rows, attention_full[s, t], NN)
            if t != 1:
                product = product + qv_biases[s, t // 2]
            products.append(product.astype(BF16))
        qkv.append(jnp.stack(products).reshape((3,) + joint_in[s].shape[:3] + (-1,)))
    attended = attention_forward(qkv[0], qkv[1])

    residual, second_norm, second_inverse, first_branch, mlp_in = [], [], [], [], []
    for s in range(2):
        product = dot(flat(attended[s]), attention_full[s, 3], NT).reshape(joint_in[s].shape)
        branch = collect(product) + proj_biases[s]
        resid = tokens[s] + mod(s, 2) * branch
        normed, inverse = layer_norm(resid)
        first_branch.append(branch)
        residual.append(resid)
        second_norm.append(normed)
        second_inverse.append(inverse)
        mlp_in.append(share((normed * (1.0 + mod(s, 4)) + mod(s, 3)).astype(BF16)))

    pre_active, active = [None, None], [None, None]
    down_rings, up_rings, last_rings = ([Ring(s, dp) for s in range(2)] for unused in range(3))
    for s in (1, 0):
        pre_active[s] = dot(flat(mlp_in[s]), up_full[s], NN) + up_biases[s]
        active[s] = gelu_tanh(pre_active[s]).astype(BF16)
        grad = dot(flat(down_up[s]), active[s], TN).astype(BF16)
        grad, down_up = tie(grad, down_up)
        down_rings[s].give(grad)

    grad_pre, back = [], []
    for s in range(2):
        grad_active = dot(flat(down_up[s]), down_full[s], NN)
        unused, pullback = jax.vjp(gelu_tanh, pre_active[s])
        grad_pre.append(pullback(grad_active)[0].astype(BF16))
        grad_pre[s] = beat(grad_pre[s], down_rings)
        back.append(dot(grad_pre[s], up_full[s], NT).reshape(mlp_in[s].shape))
        if s == 0:
            back[0], down_up[1] = beat((back[0], down_up[1]), down_rings)
            back[0] = collect(back[0])
    grad_pre, back[1] = beat((grad_pre, back[1]), down_rings)
    back[1] = collect(back[1])
    up_grad = dot(flat(mlp_in[0]), grad_pre[0], TN).astype(BF16)
    up_grad, grad_pre[1] = beat((up_grad, grad_pre[1]), down_rings)
    up_rings[0].give(up_grad)
    up_rings[1].give(dot(flat(mlp_in[1]), grad_pre[1], TN).astype(BF16))
    back = beat(back, down_rings, up_rings)

    resid_grad, attention_low = [], []
    for s in range(2):
        grad_one = cotangents[s] + norm_back(
            second_norm[s], second_inverse[s], back[s] * (1.0 + mod(s, 4))
        )
        resid_grad.append(grad_one)
        attention_low.append((grad_one * mod(s, 2)).astype(BF16))
    resid_grad, attention_low = beat((resid_grad, attention_low), down_rings, up_rings)
    active, attention_low = tie(active, attention_low)
    attention_low = [share(rows) for rows in attention_low]
    shift_two, scale_two, gate_one, proj_bias_grad = [], [], [], []
    for s in range(2):
        shift_two.append(jnp.sum(back[s], axis=1))
        scale_two.append(jnp.sum(back[s] * second_norm[s], axis=1))
        gate_one.append(jnp.sum(resid_grad[s] * first_branch[s], axis=1))
        proj_bias_grad.append(jnp.sum(resid_grad[s] * mod(s, 2), axis=(0, 1)))
    up_bias_grad = [jnp.sum(grad_pre[s].astype(F32), axis=0) for s in range(2)]
    down_sum = [None, None]
    down_sum[0] = dot(active[0], down_full[0], NT).reshape(mlp_in[0].shape)
    down_sum[0], active[1] = beat((down_sum[0], active[1]), down_rings, up_rings)
    down_sum[1] = dot(active[1], down_full[1], NT).reshape(mlp_in[1].shape)
    down_sum = beat(down_sum, down_rings, up_rings)
    attention_low, down_sum = beat((attention_low, down_sum), down_rings, up_rings)
    down_sum = [collect(down_sum[s]) for s in range(2)]

    mixed = [
        dot(flat(attention_low[s]), attention_full[s, 3], NN).astype(BF16).reshape(attended[s].shape)
        for s in range(2)
    ]
    proj_grad = [dot(flat(attention_low[s]), flat(attended[s]), TN).astype(BF16) for s in range(2)]
    mixed, proj_grad = beat((mixed, proj_grad), down_rings, up_rings)
    for s in range(2):
        last_rings[s].give(proj_grad[s])
    grad_qkv = []
    for n in range(seqs):
        piece = attention_backward(qkv[0], qkv[1], mixed[0], mixed[1], n)
        piece, mixed = beat((piece, mixed), down_rings, up_rings)
        grad_qkv.append(piece)
    grad_qkv = [jnp.concatenate([g[s] for g in grad_qkv], axis=2) for s in range(2)]
    grad_qkv, down_sum = tie(grad_qkv, down_sum)

    back, qv_bias_grad = [], []
    for s in range(2):
        grad_rows = [flat(grad_qkv[s][t]) for t in range(3)]
        total = sum(dot(grad_rows[t], attention_full[s, t], NT) for t in range(3))
        total, grad_rows = tie(total, grad_rows)
        back.append(collect(total.reshape(joint_in[s].shape)))
        for t in range(3):
            last_rings[s].give(dot(flat(joint_in[s]), grad_rows[t], TN).astype(BF16))
        qv_bias_grad.append(
            jnp.stack([jnp.sum(grad_rows[t].astype(F32), axis=0) for t in (0, 2)])
        )
    while up_rings[0].result is None:
        beat((), down_rings, up_rings)
    beat((), last_rings)
    outputs, gate_two = [], []
    for s in range(2):
        branch = down_sum[s] + down_biases[s]
        outputs.append((live * (residual[s] + mod(s, 5) * branch)).astype(BF16))
        gate_two.append(jnp.sum(cotangents[s] * branch, axis=1))
    beat((), last_rings)
    back, gate_two = tie(back, gate_two)
    shift_one, scale_one, input_grads = [], [], []
    for s in range(2):
        shift_one.append(jnp.sum(back[s], axis=1))
        scale_one.append(jnp.sum(back[s] * first_norm[s], axis=1))
        input_grads.append(
            resid_grad[s]
            + norm_back(first_norm[s], first_inverse[s], back[s] * (1.0 + mod(s, 1)))
        )

    fc1_out = jnp.stack([ring.finish() for ring in up_rings])
    fc2_out = jnp.swapaxes(jnp.stack([ring.finish() for ring in down_rings]), 1, 2)
    last = jnp.stack([ring.finish() for ring in last_rings])
    last = jnp.moveaxis(last.reshape(2, last.shape[1], 4, -1), 2, 1)
    qkv_out = last[:, 1:]
    proj_out = jnp.swapaxes(last[:, 0], 1, 2)

    mod_rows = jnp.stack(
        [
            jnp.stack([a[s] for a in (shift_one, scale_one, gate_one, shift_two, scale_two, gate_two)], axis=1)
            for s in range(2)
        ],
        axis=1,
    )
    down_bias_grad = [jnp.sum(branch_grad[s], axis=(0, 1)) for s in range(2)]
    token_sums = jnp.concatenate(
        [mod_rows.reshape(-1), jnp.stack(proj_bias_grad).reshape(-1), jnp.stack(down_bias_grad).reshape(-1)]
    ).astype(BF16)
    if mp == 2:
        token_sums = (
            token_sums.astype(F32) + lax.ppermute(token_sums, "mp", swap).astype(F32)
        ).astype(BF16)
    else:
        token_sums = lax.psum(token_sums, "mp")
    unit_sums = jnp.concatenate(
        [jnp.stack(qv_bias_grad).reshape(-1), jnp.stack(up_bias_grad).reshape(-1)]
    ).astype(BF16)
    sums = gather_vector(jnp.concatenate([token_sums, unit_sums]))
    mod_size = mod_rows.size
    bias_size = token_sums.size + unit_sums.size - mod_size
    mod_all = sums[:, :mod_size].reshape(dp * seqs, 2, 6 * width)
    totals = jnp.sum(sums[:, mod_size : mod_size + bias_size].astype(F32), axis=0)

    def own(total, axis):
        part = total.shape[axis] // dp
        return lax.dynamic_slice_in_dim(total, my_dp * part, part, axis=axis)

    at = 2 * width
    proj_bias_out = own(totals[:at].reshape(2, width), 1)
    fc2_bias_out = own(totals[at : 2 * at].reshape(2, width), 1)
    at = 2 * at
    qv_size = 4 * qv_biases.shape[2]
    qv_bias_out = own(totals[at : at + qv_size].reshape(2, 2, -1), 2)
    fc1_bias_out = own(totals[at + qv_size :].reshape(2, -1), 1)
    ada_bias_out = own(jnp.sum(mod_all.astype(F32), axis=0), 1)
    ada_out = jnp.stack([dot(silu_mine, mod_all[:, s], TN) for s in range(2)])
    silu_grad = sum(dot(mod_all[:, s], ada_low[s], NT) for s in range(2))
    silu_grad = gather_small(silu_grad[None])
    silu_grad = lax.dynamic_slice_in_dim(silu_grad, my_dp * seqs, seqs, axis=1)
    silu_grad = jnp.moveaxis(silu_grad, 0, 1).reshape(seqs, -1)
    unused, pullback = jax.vjp(jax.nn.silu, condition.astype(F32))
    cond_out = pullback(silu_grad)[0]

    return (
        outputs[0],
        outputs[1],
        ada_out,
        ada_bias_out,
        qkv_out,
        qv_bias_out,
        proj_out,
        proj_bias_out,
        fc1_out,
        fc1_bias_out,
        fc2_out,
        fc2_bias_out,
        input_grads[0],
        input_grads[1],
        cond_out,
    )


def solution(mesh):
    tokens = P("dp", "mp", None)
    weights = (
        P(None, ("mp", "dp"), None),
        P(None, "dp"),
        P(None, None, "dp", "mp"),
        P(None, None, ("mp", "dp")),
        P(None, "mp", "dp"),
        P(None, "dp"),
        P(None, "dp", "mp"),
        P(None, ("mp", "dp")),
        P(None, "mp", "dp"),
        P(None, "dp"),
    )
    return jax.shard_map(
        functools.partial(body, mesh.shape["mp"], mesh.shape["dp"]),
        mesh=mesh,
        in_specs=(tokens, tokens, P("dp", "mp"), P("dp", None)) + weights + (tokens, tokens),
        out_specs=(tokens, tokens) + weights + (tokens, tokens, P("dp", "mp")),
        check_vma=False,
    )
```

```python
import functools

import jax
import jax.numpy as jnp
from jax import lax
from jax.experimental import pallas as pl
from jax.experimental.pallas import tpu as pltpu
from jax.sharding import PartitionSpec as P

HEAD_DIM = 64
EPSILON = 1e-06
F32 = jnp.float32
BF16 = jnp.bfloat16


def gelu_pair(values):
    root, cubic = (2.0 / 3.141592653589793) ** 0.5, 0.044715
    square = values * values
    bend = jnp.tanh(root * values * (1.0 + cubic * square))
    half = 0.5 * (1.0 + bend)
    slope = half + 0.5 * values * (1.0 - bend * bend) * root * (1.0 + 3.0 * cubic * square)
    return values * half, slope


def dot(left, right, dims):
    return lax.dot_general(left, right, (dims, ((), ())), preferred_element_type=F32)


NN = ((1,), (0,))
NT = ((1,), (1,))
TN = ((0,), (0,))


def join_rows(text_ref, image_ref):
    width = text_ref.shape[-1]
    return jnp.concatenate(
        [text_ref[...].reshape(-1, width), image_ref[...].reshape(-1, width)], axis=0
    )


def parts_of(joined):
    lanes = joined.shape[1] // 3
    return [joined[:, place * lanes : (place + 1) * lanes] for place in range(3)]


def attention_kernel(image_ref, text_ref, oi, ot):
    query, key, value = parts_of(join_rows(text_ref, image_ref))
    width = query.shape[1]
    head_of = lax.broadcasted_iota(jnp.int32, query.shape, 1) // HEAD_DIM
    out = jnp.zeros(query.shape, F32)
    for head in range(width // HEAD_DIM):
        inside = head_of == head
        scores = dot(jnp.where(inside, query, jnp.zeros_like(query)), key, NT) * HEAD_DIM**-0.5
        raised = jnp.exp(scores - jnp.max(scores, axis=1, keepdims=True))
        probs = raised * (1.0 / jnp.sum(raised, axis=1, keepdims=True))
        out = jnp.where(inside, dot(probs.astype(BF16), value, NN), out)
    text_rows = ot.shape[0] * ot.shape[1]
    ot[...] = out[:text_rows].astype(BF16).reshape(ot.shape)
    oi[...] = out[text_rows:].astype(BF16).reshape(oi.shape)


def attention_back_kernel(image_ref, text_ref, gi, gt, di, dt):
    query, key, value = parts_of(join_rows(text_ref, image_ref))
    grad = join_rows(gt, gi)
    width = query.shape[1]
    head_of = lax.broadcasted_iota(jnp.int32, query.shape, 1) // HEAD_DIM
    blank = jnp.zeros_like(query)
    dq, dk, dv = (jnp.zeros(query.shape, F32) for _ in range(3))
    scale = HEAD_DIM**-0.5
    for head in range(width // HEAD_DIM):
        inside = head_of == head
        scores = dot(jnp.where(inside, key, blank), query, NT) * scale
        raised = jnp.exp(scores - jnp.max(scores, axis=0, keepdims=True))
        probs = raised * (1.0 / jnp.sum(raised, axis=0, keepdims=True))
        grad_probs = dot(jnp.where(inside, value, blank), grad, NT)
        delta = jnp.sum(probs * grad_probs, axis=0, keepdims=True)
        grad_scores = (probs * (grad_probs - delta)).astype(BF16)
        dv = jnp.where(inside, dot(probs.astype(BF16), grad, NN), dv)
        dk = jnp.where(inside, dot(grad_scores, query, NN) * scale, dk)
        dq = jnp.where(inside, dot(grad_scores, key, TN) * scale, dq)
    text_rows = dt.shape[0] * dt.shape[1]
    low = jnp.concatenate([part.astype(BF16) for part in (dq, dk, dv)], axis=1)
    dt[...] = low[:text_rows].reshape(dt.shape)
    di[...] = low[text_rows:].reshape(di.shape)


def head_block(width):
    return 128 if width % 128 == 0 else width


def blocked(shape, lanes, first=0):
    return pl.BlockSpec(
        (shape[0], None, shape[2], lanes), lambda seq, block: (0, seq + first, 0, block)
    )


VMEM = pltpu.CompilerParams(vmem_limit_bytes=48 * 2**20)
COST = pl.CostEstimate(flops=1024, transcendentals=0, bytes_accessed=1024)


def attention_forward(image, text):
    seqs, width = image.shape[1], image.shape[3] // 3
    lanes = head_block(width)
    shapes = [jax.ShapeDtypeStruct(a.shape[:3] + (width,), BF16) for a in (image, text)]
    return pl.pallas_call(
        attention_kernel,
        grid=(seqs, width // lanes),
        in_specs=[blocked(a.shape, 3 * lanes) for a in (image, text)],
        out_specs=[blocked(s.shape, lanes) for s in shapes],
        out_shape=shapes,
        compiler_params=VMEM,
        cost_estimate=COST,
        name="attention_forward",
    )(image, text)


def attention_backward(image, text, image_grad, text_grad, first, into):
    width = image.shape[3] // 3
    lanes = head_block(width)
    specs = [blocked(a.shape, 3 * lanes, first) for a in (image, text)]
    specs += [blocked(a.shape, lanes, first) for a in (image_grad, text_grad)]
    kernel = attention_back_kernel
    if into:
        specs += [pl.BlockSpec(memory_space=pl.ANY)] * 2

        def kernel(image_ref, text_ref, gi, gt, unused_image, unused_text, di, dt):
            attention_back_kernel(image_ref, text_ref, gi, gt, di, dt)

    return pl.pallas_call(
        kernel,
        grid=(1, width // lanes),
        in_specs=specs,
        out_specs=[blocked(a.shape, 3 * lanes, first) for a in (image, text)],
        out_shape=[jax.ShapeDtypeStruct(a.shape, BF16) for a in (image, text)],
        input_output_aliases={4: 0, 5: 1} if into else {},
        compiler_params=VMEM,
        cost_estimate=COST,
        name="attention_backward",
    )(image, text, image_grad, text_grad, *into)


def centred(values):
    center = values - jnp.mean(values, axis=-1, keepdims=True)
    inverse = lax.rsqrt(jnp.mean(center * center, axis=-1, keepdims=True) + EPSILON)
    return center * inverse, inverse


def norm_back(normed, inverse, upstream):
    mean_up = jnp.mean(upstream, axis=-1, keepdims=True)
    mean_cross = jnp.mean(upstream * normed, axis=-1, keepdims=True)
    return inverse * (upstream - mean_up - normed * mean_cross)


def column_sum(values):
    return jnp.sum(values, axis=0, keepdims=True)


def enter_kernel(live_ref, tokens, cot, mod, low_ref, branch_ref, sum_ref):
    live = live_ref[pl.program_id(0)].astype(F32)
    normed, unused = centred(tokens[...].astype(F32))
    low_ref[...] = (normed * (1.0 + mod[1:2]) + mod[0:1]).astype(BF16)
    branch = cot[...].astype(F32) * live * mod[5:6]
    branch_ref[...] = branch.astype(BF16)
    sum_ref[...] = column_sum(branch)


def middle_kernel(live_ref, kept, came, tokens, bias, mod, branch_ref, resid_ref, low_ref):
    branch = kept[...] + came[...].astype(F32) + bias[...]
    resid = tokens[...].astype(F32) + mod[2:3] * branch
    normed, unused = centred(resid)
    branch_ref[...] = branch
    resid_ref[...] = resid
    low_ref[...] = (normed * (1.0 + mod[4:5]) + mod[3:4]).astype(BF16)


def middle_back_kernel(
    live_ref, kept, came, cot, resid, branch, mod, grad_ref, low_ref, sum_ref, bias_ref
):
    live = live_ref[pl.program_id(0)].astype(F32)
    back = kept[...] + came[...].astype(F32)
    normed, inverse = centred(resid[...])
    grad = cot[...].astype(F32) * live + norm_back(normed, inverse, back * (1.0 + mod[4:5]))
    grad_ref[...] = grad
    low = grad * mod[2:3]
    low_ref[...] = low.astype(BF16)
    sum_ref[0:1] = column_sum(grad * branch[...])
    sum_ref[1:2] = column_sum(back)
    sum_ref[2:3] = column_sum(back * normed)
    bias_ref[...] = column_sum(low)


def leave_kernel(live_ref, kept, came, resid, cot, bias, mod, out_ref, sum_ref):
    live = live_ref[pl.program_id(0)].astype(F32)
    branch = kept[...] + came[...].astype(F32) + bias[...]
    out_ref[...] = (live * (resid[...] + mod[5:6] * branch)).astype(BF16)
    sum_ref[...] = column_sum(cot[...].astype(F32) * live * branch)


def enter_back_kernel(live_ref, kept, came, tokens, grad, mod, grad_ref, sum_ref):
    back = kept[...] + came[...].astype(F32)
    normed, inverse = centred(tokens[...].astype(F32))
    grad_ref[...] = grad[...] + norm_back(normed, inverse, back * (1.0 + mod[1:2]))
    sum_ref[0:1] = column_sum(back)
    sum_ref[1:2] = column_sum(back * normed)


def stage(kernel, live, arrays, rows, kinds, name):
    seqs, width = live.shape[0], arrays[0].shape[-1]
    specs = []
    for array in arrays:
        if array.ndim == 2:
            specs.append(pl.BlockSpec((1, width), lambda i, live_ref: (0, 0)))
        elif array.ndim == 3:
            block = (None,) + array.shape[1:]
            specs.append(pl.BlockSpec(block, lambda i, live_ref: (i, 0, 0)))
        else:
            block = (None, None) + array.shape[2:]
            specs.append(pl.BlockSpec(block, lambda i, live_ref: (0, i, 0, 0)))
    shapes = [jax.ShapeDtypeStruct((seqs, r, width), kind) for r, kind in zip(rows, kinds)]
    return pl.pallas_call(
        kernel,
        grid_spec=pltpu.PrefetchScalarGridSpec(
            num_scalar_prefetch=1,
            grid=(seqs,),
            in_specs=specs,
            out_specs=[
                pl.BlockSpec((None, r, width), lambda i, live_ref: (i, 0, 0)) for r in rows
            ],
        ),
        out_shape=shapes,
        compiler_params=VMEM,
        cost_estimate=COST,
        name=name,
    )(live, *arrays)


def pack(arrays, picks, name):
    seqs, width = arrays[0].shape[0], arrays[0].shape[2]

    def kernel(*refs):
        refs[-1][...] = jnp.concatenate(
            [refs[array][row : row + 1] for array, row in picks], axis=0
        ).astype(BF16)

    return pl.pallas_call(
        kernel,
        grid=(seqs,),
        in_specs=[pl.BlockSpec((None,) + a.shape[1:], lambda i: (i, 0, 0)) for a in arrays],
        out_specs=pl.BlockSpec((None, len(picks), width), lambda i: (i, 0, 0)),
        out_shape=jax.ShapeDtypeStruct((seqs, len(picks), width), BF16),
        compiler_params=VMEM,
        cost_estimate=COST,
        name=name,
    )(*arrays)


def whole(array):
    return [(array, array.shape[0], 0)]


def halves(array, count):
    return [(array, array.shape[0] // count, n) for n in range(count)]


def weight_grad(left, right, core, dp):
    width, columns = left[0][0].shape[1], right[0][0].shape[1]
    rows = width // dp
    chips = max(1, 384 // (2 * rows))
    block = chips * 2 * rows
    count = len(left)

    def kernel(core_ref, *refs):
        keep_ref, give_ref = refs[2 * count :]
        value = dot(refs[0][...], refs[count][...], TN)
        for n in range(1, count):
            value = value + dot(refs[n][...], refs[count + n][...], TN)
        value = value.astype(BF16).reshape(chips, 2, rows, columns)
        first = core_ref[0] == 0

        @pl.when(first)
        def unused_first():
            keep_ref[...] = value[:, 0]
            give_ref[...] = value[:, 1]

        @pl.when(jnp.logical_not(first))
        def unused_second():
            keep_ref[...] = value[:, 1]
            give_ref[...] = value[:, 0]

    specs = [
        pl.BlockSpec((depth, block), lambda i, core_ref, which=which: (which, i))
        for unused, depth, which in left
    ]
    specs += [
        pl.BlockSpec(
            (depth, columns),
            lambda i, core_ref, which=which: (which, 0),
            pipeline_mode=pl.Buffered(1),
        )
        for unused, depth, which in right
    ]
    out = pl.BlockSpec((chips, rows, columns), lambda i, core_ref: (i, 0, 0))
    return pl.pallas_call(
        kernel,
        grid_spec=pltpu.PrefetchScalarGridSpec(
            num_scalar_prefetch=1, grid=(width // block,), in_specs=specs, out_specs=[out, out]
        ),
        out_shape=[jax.ShapeDtypeStruct((dp // 2, rows, columns), BF16)] * 2,
        compiler_params=VMEM,
        cost_estimate=COST,
        name="weight_grad",
    )(core.reshape(1), *[piece[0] for piece in left + right])


def matmul(pieces, weights, stream, dims, start, size, epilogue, outs, extra, name):
    if start % 128 or size % 128:
        weights, start = weights[:, :, start : start + size], 0
    depth = weights.shape[1]
    columns = size if dims == NN else depth
    tile = next((t for t in (512, 384) if columns % t == 0), columns)
    specs = [
        pl.BlockSpec(
            (rows, array.shape[1]),
            lambda j, which=which: (which, 0),
            pipeline_mode=pl.Buffered(1),
        )
        for array, rows, which in pieces
    ]
    if dims == NN:
        specs.append(
            pl.BlockSpec((None, depth, tile), lambda j: (stream, 0, start // tile + j))
        )
    else:
        specs.append(pl.BlockSpec((None, tile, size), lambda j: (stream, j, start // size)))
    for array in extra:
        if array.ndim == 3:
            specs.append(pl.BlockSpec((None, 1, tile), lambda j: (stream, 0, j)))
        else:
            specs.append(pl.BlockSpec((array.shape[0], tile), lambda j: (0, j)))
    count = len(pieces)

    def kernel(*refs):
        extras, results = refs[count + 1 : count + 1 + len(extra)], refs[count + 1 + len(extra) :]
        at = 0
        for n, (unused, rows, which) in enumerate(pieces):
            product = dot(refs[n][...], refs[count][...], dims)
            epilogue(n, slice(at, at + rows), product, extras, results)
            at += rows

    return pl.pallas_call(
        kernel,
        grid=(columns // tile,),
        in_specs=specs,
        out_specs=[pl.BlockSpec((rows, tile), lambda j: (0, j)) for rows, unused in outs],
        out_shape=[jax.ShapeDtypeStruct((rows, columns), kind) for rows, kind in outs],
        compiler_params=VMEM,
        cost_estimate=COST,
        name=name,
    )(*[piece[0] for piece in pieces], weights, *extra)


def low_of(n, rows, product, extras, results):
    results[0][rows] = product.astype(BF16)


def low_biased(n, rows, product, extras, results):
    results[0][rows] = (product + extras[0][...]).astype(BF16)


def gelu_biased(n, rows, product, extras, results):
    value, slope = gelu_pair(product + extras[0][...])
    results[0][rows] = value.astype(BF16)
    results[1][rows] = slope


def sloped(n, rows, product, extras, results):
    low = (product * extras[0][rows]).astype(BF16)
    results[0][rows] = low
    total = column_sum(low.astype(F32))
    results[1][...] = total if n == 0 else results[1][...] + total


def apart(n, rows, product, extras, results):
    results[n][...] = product.astype(results[n].dtype)


def ring_of(chips):
    wide = 1
    while (2 * wide) ** 2 <= chips:
        wide *= 2
    long = chips // wide
    order = [row * wide for row in range(long)]
    for turn, row in enumerate(reversed(range(long))):
        across = list(range(1, wide))
        order += [row * wide + col for col in (across if turn % 2 == 0 else across[::-1])]
    return order


class Rings:
    def __init__(self, dp, kind=BF16):
        self.kind, self.dp = kind, dp
        self.chips = dp // 2
        order = ring_of(self.chips)
        me = lax.axis_index("dp")
        chip, self.core = me // 2, me % 2
        self.hops, self.targets = [], []
        for way in (1, -1):
            self.hops.append(
                [
                    (2 * order[i] + c, 2 * order[(i + way) % self.chips] + c)
                    for i in range(self.chips)
                    for c in range(2)
                ]
            )
            targets = []
            for step in range(self.chips):
                at = jnp.int32(0)
                for spot, here in enumerate(order):
                    goal = order[(spot - way * (1 + step)) % self.chips]
                    at = at + jnp.where(chip == here, goal, 0)
                targets.append(at)
            self.targets.append(targets)
        self.views, self.flying = ([], []), ([], [])
        self.step = 0
        self.result = None

    def give(self, stream, keep, gift):
        self.views[stream].append(keep)
        swap = [(i, i ^ 1) for i in range(self.dp)]
        self.flying[stream].append(lax.ppermute(gift, "dp", swap))

    def add(self, came):
        last = self.step == self.chips - 1
        widths = [view.shape[-1] for view in self.views[0]]
        rows = self.views[0][0].shape[1]
        tile = rows // 3 if rows % 48 == 0 else rows
        at = jnp.stack([self.targets[s][self.step] for s in range(2)])
        operands, specs, places = [], [], []
        for s in range(2):
            for view, got in zip(self.views[s], self.got[s]):
                width = view.shape[-1]
                operands += [view, got]
                block = pl.BlockSpec((None, tile, width), lambda i, at, s=s: (at[s], i, 0))
                specs += [block, block]
            if came is not None:
                operands.append(came[s])
                specs.append(pl.BlockSpec((tile, sum(widths)), lambda i, at: (i, 0)))
        sizes = widths if last else [sum(widths)]
        kind = F32 if last else self.kind
        shapes = [jax.ShapeDtypeStruct((rows, size), kind) for size in sizes] * 2

        def kernel(at_ref, *refs):
            ins, outs = refs[: len(operands)], refs[len(operands) :]
            per_way = len(operands) // 2
            for s in range(2):
                mine = ins[s * per_way : (s + 1) * per_way]
                start = 0
                for number, width in enumerate(widths):
                    value = mine[2 * number][...].astype(F32) + mine[2 * number + 1][...].astype(F32)
                    if came is not None:
                        value = value + mine[-1][:, start : start + width].astype(F32)
                    if last:
                        outs[s * len(sizes) + number][...] = value
                    else:
                        outs[s][:, start : start + width] = value.astype(kind)
                    start += width

        out = pl.pallas_call(
            kernel,
            grid_spec=pltpu.PrefetchScalarGridSpec(
                num_scalar_prefetch=1,
                grid=(rows // tile,),
                in_specs=specs,
                out_specs=[
                    pl.BlockSpec((tile, shape.shape[1]), lambda i, at: (i, 0)) for shape in shapes
                ],
            ),
            out_shape=shapes,
            compiler_params=VMEM,
            cost_estimate=COST,
            name="ring_add",
        )(at, *operands)
        return [out[s * len(sizes) : (s + 1) * len(sizes)] for s in range(2)]

    def advance(self):
        if self.step == 0:
            self.got = self.flying
            total = self.add(None)
        else:
            total = self.add([flight[0] for flight in self.flying])
        self.sent = total
        if self.step == self.chips - 1:
            self.result = total
            self.flying = ([], [])
        else:
            self.flying = tuple(
                [lax.ppermute(total[s][0], "dp", self.hops[s])] for s in range(2)
            )
        self.step += 1

    def finish(self):
        while self.result is None:
            self.advance()
        return self.result


def beat(value, rings):
    if rings.result is None:
        value, rings.flying = lax.optimization_barrier((value, rings.flying))
        rings.advance()
        value, unused = lax.optimization_barrier((value, rings.sent))
    return value


def tie(*values):
    return lax.optimization_barrier(values)


def body(
    mp,
    dp,
    image_tokens,
    text_tokens,
    condition,
    live_table,
    ada_weight,
    ada_bias,
    qkv_weight,
    qv_bias,
    proj_weight,
    proj_bias,
    fc1_weight,
    fc1_bias,
    fc2_weight,
    fc2_bias,
    image_cotangent,
    text_cotangent,
):
    seqs, width = image_tokens.shape[0], image_tokens.shape[2]
    my_dp = lax.axis_index("dp")
    swap = [(0, 1), (1, 0)]

    def share(rows):
        if mp == 2:
            return whole(flat(rows)) + whole(flat(lax.ppermute(rows, "mp", swap)))
        return whole(flat(lax.all_gather(rows, "mp", axis=0, tiled=False)))

    def split(array):
        return halves(array, 2 if mp == 2 else 1)

    def collect(array, weights, stream, start, size, name):
        pieces = split(array)
        outs = [(piece[1], kind) for piece, kind in zip(pieces, (F32, BF16))]
        parts = matmul(pieces, weights, stream, NT, start, size, apart, outs, [], name)
        if mp == 2:
            shape = (1, seqs, -1, width)
            return [parts[0].reshape(shape), parts[1].reshape(shape[1:])]

        low = parts[0].astype(BF16).reshape(mp, seqs, -1, width)
        return [low, low[0]]

    def exchange(parts):
        if mp == 2:
            return parts[0], lax.ppermute(parts[1], "mp", swap)
        low = lax.psum_scatter(parts[0], "mp", scatter_dimension=0, tiled=False)
        return low.astype(F32), jnp.zeros_like(low)

    def sum_mp(values):
        if mp == 2:
            return values + lax.ppermute(values, "mp", swap)
        return lax.psum(values, "mp")

    def flat(array):
        return array.reshape(-1, array.shape[-1])

    def gather_small(rows, after=lambda rows: rows):
        shape, reach, bits = rows.shape, dp // 2, 0
        while reach >= 1:
            other = lax.ppermute(rows, "dp", [(i, i ^ reach) for i in range(dp)])
            low_half = (my_dp & reach) == 0
            rows = jnp.concatenate(
                [jnp.where(low_half, rows, other), jnp.where(low_half, other, rows)], axis=0
            )
            rows = after(rows)
            reach, bits = reach // 2, bits + 1
        rows = rows.reshape((2,) * bits + shape)
        order = tuple(reversed(range(bits))) + tuple(range(bits, bits + len(shape)))
        return rows.transpose(order).reshape((dp,) + shape)

    small = [condition, ada_bias, qv_bias, proj_bias, fc1_bias, fc2_bias]
    sizes = [a.size for a in small]
    packed = jnp.concatenate([a.astype(BF16).reshape(-1) for a in small])
    packed = jnp.pad(packed, (0, -packed.size % 2048)).reshape(-1, 128)
    packed = gather_small(packed).reshape(dp, -1)
    pieces, at = [], 0
    for array, size in zip(small, sizes):
        pieces.append(packed[:, at : at + size].reshape((dp,) + array.shape))
        at += size
    cond_all = pieces[0].reshape(dp * seqs, -1)
    ada_biases, proj_biases, up_biases, down_biases = (
        jnp.moveaxis(pieces[i], 0, 1).reshape(2, -1).astype(F32) for i in (1, 3, 4, 5)
    )
    qv_biases = jnp.moveaxis(pieces[2], 0, 2).reshape(2, 2, -1).astype(F32)

    share_rows, heads_width = qkv_weight.shape[2:]
    lanes = head_block(heads_width)
    qkv_low = qkv_weight.astype(BF16).reshape(2, 3, share_rows, -1, lanes)
    qkv_low = qkv_low.transpose(0, 2, 3, 1, 4).reshape(2, share_rows, -1)
    proj_low = jnp.swapaxes(proj_weight.astype(BF16), 1, 2)
    attention_full = lax.all_gather(
        jnp.concatenate([qkv_low, proj_low], axis=2), "dp", axis=1, tiled=True
    )
    qkv_size = 3 * heads_width
    up_full = lax.all_gather(fc1_weight.astype(BF16), "dp", axis=1, tiled=True)
    down_full = lax.all_gather(
        jnp.swapaxes(fc2_weight.astype(BF16), 1, 2), "dp", axis=1, tiled=True
    )
    biases = qv_biases.reshape(2, 2, -1, lanes)
    biases = jnp.stack([biases[:, 0], jnp.zeros_like(biases[:, 0]), biases[:, 1]], axis=2)
    biases = biases.reshape(2, 1, -1)

    ada_low = ada_weight.astype(BF16)
    ada_rows = ada_low.shape[1]
    silu_all = jax.nn.silu(cond_all.astype(F32)).astype(BF16)
    silu_mine = lax.dynamic_slice_in_dim(silu_all, my_dp * ada_rows, ada_rows, axis=1)
    core = lax.rem(my_dp, 2)
    mod_rings = Rings(dp, F32)
    for s in range(2):
        partial = dot(silu_mine, ada_low[s], NN).reshape(dp // 2, 2, -1, 128)
        keep, gift = (lax.dynamic_index_in_dim(partial, c, 1, False) for c in (core, 1 - core))
        mod_rings.give(s, keep, gift)
    modulation = jnp.stack([part[0].reshape(seqs, -1) for part in mod_rings.finish()], axis=1)
    modulation = (sum_mp(modulation) + ada_biases).reshape(seqs, 2, 6, width)
    mod = [modulation[:, s] for s in range(2)]
    live = live_table[0]
    tokens, cotangents = (image_tokens, text_tokens), (image_cotangent, text_cotangent)
    rows_of = [t.shape[1] for t in tokens]

    joint_in, branch_low, branch_sum = [], [], []
    for s in range(2):
        low, branch, total = stage(
            enter_kernel,
            live,
            [tokens[s], cotangents[s], mod[s]],
            [rows_of[s], rows_of[s], 1],
            [BF16, BF16, F32],
            "enter",
        )
        joint_in.append(share(low))
        branch_low.append(branch)
        branch_sum.append(total)
    branch_low, joint_in = tie(branch_low, [[piece[0] for piece in pieces] for pieces in joint_in])
    joint_in = [[piece for array in arrays for piece in whole(array)] for arrays in joint_in]
    down_up = [share(branch_low[s]) for s in range(2)]
    all_rows = [mp * seqs * rows_of[s] for s in range(2)]
    units = up_biases.shape[1]

    qkv = []
    for s in range(2):
        (product,) = matmul(
            joint_in[s],
            attention_full,
            s,
            NN,
            0,
            qkv_size,
            low_biased,
            [(all_rows[s], BF16)],
            [biases],
            "qkv",
        )
        qkv.append(product.reshape(mp, seqs, rows_of[s], -1))
    attended, arrived = tie(
        attention_forward(qkv[0], qkv[1]), [[piece[0] for piece in pieces] for pieces in down_up]
    )
    attended = [flat(o) for o in attended]
    down_up = [[piece for array in arrays for piece in whole(array)] for arrays in arrived]

    residual, first_branch, mlp_in = [None, None], [None, None], [None, None]
    sums = []
    for s in range(2):
        parts = collect(attended[s], attention_full, s, qkv_size, heads_width, "proj")
        sums.append(exchange(parts))
    for s in (1, 0):
        first_branch[s], residual[s], low = stage(
            middle_kernel,
            live,
            [*sums[s], tokens[s], proj_biases[s : s + 1], mod[s]],
            [rows_of[s]] * 3,
            [F32, F32, BF16],
            "middle",
        )
        mlp_in[s] = share(low)

    slope, active = [None, None], [None, None]
    rings, last_rings = Rings(dp), Rings(dp)
    up_bias_rows = up_biases.reshape(2, 1, -1)
    for s in (1, 0):
        active[s], slope[s] = matmul(
            mlp_in[s],
            up_full,
            s,
            NN,
            0,
            units,
            gelu_biased,
            [(all_rows[s], BF16), (all_rows[s], F32)],
            [up_bias_rows],
            "up",
        )
        keep, gift = weight_grad(down_up[s], split(active[s]), core, dp)
        keep, gift, slope = tie(keep, gift, slope)
        rings.give(s, keep, gift)

    grad_pre, back, up_sums = [], [], []
    for s in range(2):
        low, total = matmul(
            down_up[s],
            down_full,
            s,
            NN,
            0,
            units,
            sloped,
            [(all_rows[s], BF16), (1, F32)],
            [slope[s]],
            "down_back",
        )
        grad_pre.append(low)
        up_sums.append(total)
        back.append(collect(low, up_full, s, 0, units, "up_back"))
        back[s], slope, grad_pre = tie(back[s], slope, grad_pre)
        back[s] = exchange(back[s])
    keep, gift = weight_grad(mlp_in[0], split(grad_pre[0]), core, dp)
    keep, gift, grad_pre, back[0] = tie(keep, gift, grad_pre, back[0])
    rings.give(0, keep, gift)
    keep, gift = weight_grad(mlp_in[1], split(grad_pre[1]), core, dp)
    keep, gift, back[1] = tie(keep, gift, back[1])
    rings.give(1, keep, gift)
    back = beat(back, rings)
    back, unused = tie(back, rings.sent)

    resid_grad, attention_low, middle_sums, proj_sums = [], [], [], []
    for s in range(2):
        grad, low, total, bias_total = stage(
            middle_back_kernel,
            live,
            [*back[s], cotangents[s], residual[s], first_branch[s], mod[s]],
            [rows_of[s], rows_of[s], 3, 1],
            [F32, BF16, F32, F32],
            "middle_back",
        )
        resid_grad.append(grad)
        attention_low.append(low)
        middle_sums.append(total)
        proj_sums.append(bias_total)
    attention_low, active, middle_sums = tie(attention_low, active, middle_sums)
    attention_low = [share(rows) for rows in attention_low]
    active = beat(active, rings)
    down_sum = [collect(active[s], down_full, s, 0, units, "down") for s in range(2)]
    down_sum, middle_sums = beat((down_sum, middle_sums), rings)

    arrived, down_sum = tie([[piece[0] for piece in pieces] for pieces in attention_low], down_sum)
    attention_low = [[piece for array in arrays for piece in whole(array)] for arrays in arrived]
    down_sum = [exchange(down_sum[s]) for s in range(2)]

    mixed = []
    for s in range(2):
        (product,) = matmul(
            attention_low[s],
            attention_full,
            s,
            NN,
            qkv_size,
            heads_width,
            low_of,
            [(all_rows[s], BF16)],
            [],
            "proj_back",
        )
        mixed.append(product.reshape(mp, seqs, rows_of[s], -1))
    mixed, attended = beat((mixed, attended), rings)
    for s in range(2):
        keep, gift = weight_grad(attention_low[s], split(attended[s]), core, dp)
        keep, gift, mixed, attended = tie(keep, gift, mixed, attended)
        last_rings.give(s, keep, gift)
    grad_qkv = ()
    for n in range(seqs):
        grad_qkv = attention_backward(qkv[0], qkv[1], mixed[0], mixed[1], n, grad_qkv)
        if n == 1:
            grad_qkv, mixed, last_rings.flying, down_sum = tie(
                grad_qkv, mixed, last_rings.flying, down_sum
            )
        else:
            grad_qkv, mixed = beat((grad_qkv, mixed), rings)
    grad_qkv = [flat(g) for g in grad_qkv]

    back = [None, None]
    for s in range(2):
        back[s] = collect(grad_qkv[s], attention_full, s, 0, qkv_size, "qkv_back")
        back[s], grad_qkv = tie(back[s], grad_qkv)
        back[s] = exchange(back[s])
    for s in range(2):
        keep, gift = weight_grad(joint_in[s], split(grad_qkv[s]), core, dp)
        keep, gift, grad_qkv = tie(keep, gift, grad_qkv)
        last_rings.give(s, keep, gift)
    down_sum, grad_qkv = beat((down_sum, grad_qkv), last_rings)
    outputs, gate_two = [], []
    for s in range(2):
        out, total = stage(
            leave_kernel,
            live,
            [*down_sum[s], residual[s], cotangents[s], down_biases[s : s + 1], mod[s]],
            [rows_of[s], 1],
            [BF16, F32],
            "leave",
        )
        outputs.append(out)
        gate_two.append(total)
    qv_sums = []
    for s in range(2):
        total = jnp.sum(grad_qkv[s].astype(F32), axis=0).reshape(-1, 3, lanes)
        qv_sums += [total[:, 0], total[:, 2]]
    unit_sums = jnp.concatenate([u.reshape(-1) for u in qv_sums + up_sums])
    unit_size = unit_sums.size
    unit_sums = jnp.pad(unit_sums, (0, -unit_size % (seqs * width))).reshape(seqs, -1, width)
    unit_rows = unit_sums.shape[1]
    gate_two, unit_sums = beat((gate_two, unit_sums), rings)
    back, gate_two, unit_sums = tie(back, gate_two, unit_sums)

    input_grads, first_sums = [], []
    for s in range(2):
        grad, total = stage(
            enter_back_kernel,
            live,
            [*back[s], tokens[s], resid_grad[s], mod[s]],
            [rows_of[s], 2],
            [F32, F32],
            "enter_back",
        )
        input_grads.append(grad)
        first_sums.append(total)
    packed_sums, picks = [], []
    for s in range(2):
        at = len(packed_sums)
        packed_sums += [first_sums[s], middle_sums[s], gate_two[s]]
        picks += [(at, 0), (at, 1)] + [(at + 1, row) for row in range(3)] + [(at + 2, 0)]
    for array in proj_sums + branch_sum:
        picks.append((len(packed_sums), 0))
        packed_sums.append(array)
    token_rows = len(picks)
    picks += [(len(packed_sums), row) for row in range(unit_rows)]
    sums = pack(packed_sums + [unit_sums], picks, "pack")
    sums, input_grads = tie(sums, input_grads)
    if mp == 2:
        other = lax.ppermute(sums, "mp", swap)
        row_of = lax.broadcasted_iota(jnp.int32, sums.shape, 1)
        other = jnp.where(row_of < token_rows, other.astype(F32), 0.0)
        sums = (sums.astype(F32) + other).astype(BF16)
    else:
        sums = jnp.concatenate(
            [lax.psum(sums[:, :token_rows], "mp"), sums[:, token_rows:]], axis=1
        )
    gathered = lax.all_gather(sums, "dp", axis=0, tiled=True)
    input_grads = beat(input_grads, last_rings)
    while rings.result is None:
        input_grads = beat(input_grads, rings)
    input_grads = beat(input_grads, last_rings)
    fc2_out, fc1_out = (jnp.stack([part[n] for part in rings.finish()]) for n in range(2))
    fc2_out = jnp.swapaxes(fc2_out, 1, 2)
    fc1_out = beat(fc1_out, last_rings)
    fc2_out = beat(fc2_out, last_rings)
    gathered = beat(gathered, last_rings)

    mod_all = [gathered[:, 6 * s : 6 * s + 6].reshape(dp * seqs, 6 * width) for s in range(2)]
    silu_grad = sum(dot(mod_all[s], ada_low[s], NT) for s in range(2))
    silu_grad = gather_small(silu_grad, lambda rows: beat(rows, last_rings))
    silu_grad, gathered = tie(silu_grad, gathered)
    silu_grad = lax.dynamic_slice_in_dim(silu_grad, my_dp * seqs, seqs, axis=1)
    silu_grad = jnp.moveaxis(silu_grad, 0, 1).reshape(seqs, -1)
    unused, pullback = jax.vjp(jax.nn.silu, condition.astype(F32))
    cond_out = pullback(silu_grad)[0]
    bias_all = jnp.sum(gathered[:, 12:token_rows].astype(F32), axis=0)
    unit_all = jnp.sum(gathered[:, token_rows:].astype(F32).reshape(dp, -1), axis=0)
    qv_size = qv_biases.size

    proj_out, qkv_out = (jnp.stack([part[n] for part in last_rings.finish()]) for n in range(2))
    proj_out = jnp.swapaxes(proj_out, 1, 2)
    qkv_out = qkv_out.reshape(2, share_rows, -1, 3, lanes)
    qkv_out = qkv_out.transpose(0, 3, 1, 2, 4).reshape(qkv_weight.shape)

    def own(total, axis):
        part = total.shape[axis] // dp
        return lax.dynamic_slice_in_dim(total, my_dp * part, part, axis=axis)

    proj_bias_out = own(bias_all[0:2], 1)
    fc2_bias_out = own(bias_all[2:4], 1)
    fc1_bias_out = own(unit_all[qv_size:unit_size].reshape(2, -1), 1)
    qv_bias_out = own(unit_all[:qv_size].reshape(qv_biases.shape), 2)
    ada_bias_out = own(jnp.stack([jnp.sum(m.astype(F32), axis=0) for m in mod_all]), 1)
    ada_out = jnp.stack([dot(silu_mine, mod_all[s], TN) for s in range(2)])

    return (
        outputs[0],
        outputs[1],
        ada_out,
        ada_bias_out,
        qkv_out,
        qv_bias_out,
        proj_out,
        proj_bias_out,
        fc1_out,
        fc1_bias_out,
        fc2_out,
        fc2_bias_out,
        input_grads[0],
        input_grads[1],
        cond_out,
    )


def solution(mesh):
    tokens = P("dp", "mp", None)
    weights = (
        P(None, ("mp", "dp"), None),
        P(None, "dp"),
        P(None, None, "dp", "mp"),
        P(None, None, ("mp", "dp")),
        P(None, "mp", "dp"),
        P(None, "dp"),
        P(None, "dp", "mp"),
        P(None, ("mp", "dp")),
        P(None, "mp", "dp"),
        P(None, "dp"),
    )
    return jax.shard_map(
        functools.partial(body, mesh.shape["mp"], mesh.shape["dp"]),
        mesh=mesh,
        in_specs=(tokens, tokens, P("dp", "mp"), P("dp", None)) + weights + (tokens, tokens),
        out_specs=(tokens, tokens) + weights + (tokens, tokens, P("dp", "mp")),
        check_vma=False,
    )
```

```python
import functools

import jax
import jax.numpy as jnp
from jax import lax
from jax.experimental import pallas as pl
from jax.experimental.pallas import tpu as pltpu
from jax.sharding import PartitionSpec as P

HEAD_DIM = 64
EPSILON = 1e-06
F32 = jnp.float32
BF16 = jnp.bfloat16


def gelu_pair(values):
    root, cubic = (2.0 / 3.141592653589793) ** 0.5, 0.044715
    square = values * values
    bend = jnp.tanh(root * values * (1.0 + cubic * square))
    half = 0.5 * (1.0 + bend)
    slope = half + 0.5 * values * (1.0 - bend * bend) * root * (1.0 + 3.0 * cubic * square)
    return values * half, slope


def dot(left, right, dims):
    return lax.dot_general(left, right, (dims, ((), ())), preferred_element_type=F32)


NN = ((1,), (0,))
NT = ((1,), (1,))
TN = ((0,), (0,))


def join_rows(text_ref, image_ref):
    width = text_ref.shape[-1]
    return jnp.concatenate(
        [text_ref[...].reshape(-1, width), image_ref[...].reshape(-1, width)], axis=0
    )


def parts_of(joined):
    lanes = joined.shape[1] // 3
    return [joined[:, place * lanes : (place + 1) * lanes] for place in range(3)]


def attention_kernel(image_ref, text_ref, oi, ot):
    query, key, value = parts_of(join_rows(text_ref, image_ref))
    width = query.shape[1]
    head_of = lax.broadcasted_iota(jnp.int32, query.shape, 1) // HEAD_DIM
    out = jnp.zeros(query.shape, F32)
    for head in range(width // HEAD_DIM):
        inside = head_of == head
        scores = dot(jnp.where(inside, query, jnp.zeros_like(query)), key, NT) * HEAD_DIM**-0.5
        raised = jnp.exp(scores - jnp.max(scores, axis=1, keepdims=True))
        probs = raised * (1.0 / jnp.sum(raised, axis=1, keepdims=True))
        out = jnp.where(inside, dot(probs.astype(BF16), value, NN), out)
    text_rows = ot.shape[0] * ot.shape[1]
    ot[...] = out[:text_rows].astype(BF16).reshape(ot.shape)
    oi[...] = out[text_rows:].astype(BF16).reshape(oi.shape)


def attention_back_kernel(image_ref, text_ref, gi, gt, di, dt):
    query, key, value = parts_of(join_rows(text_ref, image_ref))
    grad = join_rows(gt, gi)
    width = query.shape[1]
    head_of = lax.broadcasted_iota(jnp.int32, query.shape, 1) // HEAD_DIM
    blank = jnp.zeros_like(query)
    dq, dk, dv = (jnp.zeros(query.shape, F32) for _ in range(3))
    scale = HEAD_DIM**-0.5
    for head in range(width // HEAD_DIM):
        inside = head_of == head
        scores = dot(jnp.where(inside, key, blank), query, NT) * scale
        raised = jnp.exp(scores - jnp.max(scores, axis=0, keepdims=True))
        probs = raised * (1.0 / jnp.sum(raised, axis=0, keepdims=True))
        grad_probs = dot(jnp.where(inside, value, blank), grad, NT)
        delta = jnp.sum(probs * grad_probs, axis=0, keepdims=True)
        grad_scores = (probs * (grad_probs - delta)).astype(BF16)
        dv = jnp.where(inside, dot(probs.astype(BF16), grad, NN), dv)
        dk = jnp.where(inside, dot(grad_scores, query, NN) * scale, dk)
        dq = jnp.where(inside, dot(grad_scores, key, TN) * scale, dq)
    text_rows = dt.shape[0] * dt.shape[1]
    low = jnp.concatenate([part.astype(BF16) for part in (dq, dk, dv)], axis=1)
    dt[...] = low[:text_rows].reshape(dt.shape)
    di[...] = low[text_rows:].reshape(di.shape)


def head_block(width):
    return 128 if width % 128 == 0 else width


def blocked(shape, lanes, first=0):
    return pl.BlockSpec(
        (shape[0], None, shape[2], lanes), lambda seq, block: (0, seq + first, 0, block)
    )


VMEM = pltpu.CompilerParams(vmem_limit_bytes=48 * 2**20)
COST = pl.CostEstimate(flops=1024, transcendentals=0, bytes_accessed=1024)


def attention_forward(image, text):
    seqs, width = image.shape[1], image.shape[3] // 3
    lanes = head_block(width)
    shapes = [jax.ShapeDtypeStruct(a.shape[:3] + (width,), BF16) for a in (image, text)]
    return pl.pallas_call(
        attention_kernel,
        grid=(seqs, width // lanes),
        in_specs=[blocked(a.shape, 3 * lanes) for a in (image, text)],
        out_specs=[blocked(s.shape, lanes) for s in shapes],
        out_shape=shapes,
        compiler_params=VMEM,
        cost_estimate=COST,
        name="attention_forward",
    )(image, text)


def attention_backward(image, text, image_grad, text_grad, first, into):
    width = image.shape[3] // 3
    lanes = head_block(width)
    specs = [blocked(a.shape, 3 * lanes, first) for a in (image, text)]
    specs += [blocked(a.shape, lanes, first) for a in (image_grad, text_grad)]
    kernel = attention_back_kernel
    if into:
        specs += [pl.BlockSpec(memory_space=pl.ANY)] * 2

        def kernel(image_ref, text_ref, gi, gt, unused_image, unused_text, di, dt):
            attention_back_kernel(image_ref, text_ref, gi, gt, di, dt)

    return pl.pallas_call(
        kernel,
        grid=(1, width // lanes),
        in_specs=specs,
        out_specs=[blocked(a.shape, 3 * lanes, first) for a in (image, text)],
        out_shape=[jax.ShapeDtypeStruct(a.shape, BF16) for a in (image, text)],
        input_output_aliases={4: 0, 5: 1} if into else {},
        compiler_params=VMEM,
        cost_estimate=COST,
        name="attention_backward",
    )(image, text, image_grad, text_grad, *into)


def centred(values):
    center = values - jnp.mean(values, axis=-1, keepdims=True)
    inverse = lax.rsqrt(jnp.mean(center * center, axis=-1, keepdims=True) + EPSILON)
    return center * inverse, inverse


def norm_back(normed, inverse, upstream):
    mean_up = jnp.mean(upstream, axis=-1, keepdims=True)
    mean_cross = jnp.mean(upstream * normed, axis=-1, keepdims=True)
    return inverse * (upstream - mean_up - normed * mean_cross)


def column_sum(values):
    return jnp.sum(values, axis=0, keepdims=True)


def enter_kernel(live_ref, tokens, cot, mod, low_ref, branch_ref, sum_ref):
    live = live_ref[pl.program_id(0)].astype(F32)
    normed, unused = centred(tokens[...].astype(F32))
    low_ref[...] = (normed * (1.0 + mod[1:2]) + mod[0:1]).astype(BF16)
    branch = cot[...].astype(F32) * live * mod[5:6]
    branch_ref[...] = branch.astype(BF16)
    sum_ref[...] = column_sum(branch)


def middle_kernel(live_ref, kept, came, tokens, bias, mod, branch_ref, resid_ref, low_ref):
    branch = kept[...] + came[...].astype(F32) + bias[...]
    resid = tokens[...].astype(F32) + mod[2:3] * branch
    normed, unused = centred(resid)
    branch_ref[...] = branch
    resid_ref[...] = resid
    low_ref[...] = (normed * (1.0 + mod[4:5]) + mod[3:4]).astype(BF16)


def middle_back_kernel(
    live_ref, kept, came, cot, resid, branch, mod, grad_ref, low_ref, sum_ref, bias_ref
):
    live = live_ref[pl.program_id(0)].astype(F32)
    back = kept[...] + came[...].astype(F32)
    normed, inverse = centred(resid[...])
    grad = cot[...].astype(F32) * live + norm_back(normed, inverse, back * (1.0 + mod[4:5]))
    grad_ref[...] = grad
    low = grad * mod[2:3]
    low_ref[...] = low.astype(BF16)
    sum_ref[0:1] = column_sum(grad * branch[...])
    sum_ref[1:2] = column_sum(back)
    sum_ref[2:3] = column_sum(back * normed)
    bias_ref[...] = column_sum(low)


def leave_kernel(live_ref, kept, came, resid, cot, bias, mod, out_ref, sum_ref):
    live = live_ref[pl.program_id(0)].astype(F32)
    branch = kept[...] + came[...].astype(F32) + bias[...]
    out_ref[...] = (live * (resid[...] + mod[5:6] * branch)).astype(BF16)
    sum_ref[...] = column_sum(cot[...].astype(F32) * live * branch)


def enter_back_kernel(live_ref, kept, came, tokens, grad, mod, grad_ref, sum_ref):
    back = kept[...] + came[...].astype(F32)
    normed, inverse = centred(tokens[...].astype(F32))
    grad_ref[...] = grad[...] + norm_back(normed, inverse, back * (1.0 + mod[1:2]))
    sum_ref[0:1] = column_sum(back)
    sum_ref[1:2] = column_sum(back * normed)


def stage(kernel, live, arrays, rows, kinds, name):
    seqs, width = live.shape[0], arrays[0].shape[-1]
    specs = []
    for array in arrays:
        if array.ndim == 2:
            specs.append(pl.BlockSpec((1, width), lambda i, live_ref: (0, 0)))
        elif array.ndim == 3:
            block = (None,) + array.shape[1:]
            specs.append(pl.BlockSpec(block, lambda i, live_ref: (i, 0, 0)))
        else:
            block = (None, None) + array.shape[2:]
            specs.append(pl.BlockSpec(block, lambda i, live_ref: (0, i, 0, 0)))
    shapes = [jax.ShapeDtypeStruct((seqs, r, width), kind) for r, kind in zip(rows, kinds)]
    return pl.pallas_call(
        kernel,
        grid_spec=pltpu.PrefetchScalarGridSpec(
            num_scalar_prefetch=1,
            grid=(seqs,),
            in_specs=specs,
            out_specs=[
                pl.BlockSpec((None, r, width), lambda i, live_ref: (i, 0, 0)) for r in rows
            ],
        ),
        out_shape=shapes,
        compiler_params=VMEM,
        cost_estimate=COST,
        name=name,
    )(live, *arrays)


def pack(arrays, picks, name):
    seqs, width = arrays[0].shape[0], arrays[0].shape[2]

    def kernel(*refs):
        refs[-1][...] = jnp.concatenate(
            [refs[array][row : row + 1] for array, row in picks], axis=0
        ).astype(BF16)

    return pl.pallas_call(
        kernel,
        grid=(seqs,),
        in_specs=[pl.BlockSpec((None,) + a.shape[1:], lambda i: (i, 0, 0)) for a in arrays],
        out_specs=pl.BlockSpec((None, len(picks), width), lambda i: (i, 0, 0)),
        out_shape=jax.ShapeDtypeStruct((seqs, len(picks), width), BF16),
        compiler_params=VMEM,
        cost_estimate=COST,
        name=name,
    )(*arrays)


def whole(array):
    return [(array, array.shape[0], 0)]


def halves(array, count):
    return [(array, array.shape[0] // count, n) for n in range(count)]


def weight_grad(left, right, core, dp):
    width, columns = left[0][0].shape[1], right[0][0].shape[1]
    rows = width // dp
    chips = max(1, 384 // (2 * rows))
    block = chips * 2 * rows
    count = len(left)

    def kernel(core_ref, *refs):
        keep_ref, give_ref = refs[2 * count :]
        value = dot(refs[0][...], refs[count][...], TN)
        for n in range(1, count):
            value = value + dot(refs[n][...], refs[count + n][...], TN)
        value = value.astype(BF16).reshape(chips, 2, rows, columns)
        first = core_ref[0] == 0

        @pl.when(first)
        def unused_first():
            keep_ref[...] = value[:, 0]
            give_ref[...] = value[:, 1]

        @pl.when(jnp.logical_not(first))
        def unused_second():
            keep_ref[...] = value[:, 1]
            give_ref[...] = value[:, 0]

    specs = [
        pl.BlockSpec((depth, block), lambda i, core_ref, which=which: (which, i))
        for unused, depth, which in left
    ]
    specs += [
        pl.BlockSpec(
            (depth, columns),
            lambda i, core_ref, which=which: (which, 0),
            pipeline_mode=pl.Buffered(1),
        )
        for unused, depth, which in right
    ]
    out = pl.BlockSpec((chips, rows, columns), lambda i, core_ref: (i, 0, 0))
    return pl.pallas_call(
        kernel,
        grid_spec=pltpu.PrefetchScalarGridSpec(
            num_scalar_prefetch=1, grid=(width // block,), in_specs=specs, out_specs=[out, out]
        ),
        out_shape=[jax.ShapeDtypeStruct((dp // 2, rows, columns), BF16)] * 2,
        compiler_params=VMEM,
        cost_estimate=COST,
        name="weight_grad",
    )(core.reshape(1), *[piece[0] for piece in left + right])


def matmul(pieces, weights, stream, dims, start, size, epilogue, outs, extra, name):
    if start % 128 or size % 128:
        weights, start = weights[:, :, start : start + size], 0
    depth = weights.shape[1]
    columns = size if dims == NN else depth
    tile = next((t for t in (512, 384) if columns % t == 0), columns)
    specs = [
        pl.BlockSpec(
            (rows, array.shape[1]),
            lambda j, which=which: (which, 0),
            pipeline_mode=pl.Buffered(1),
        )
        for array, rows, which in pieces
    ]
    if dims == NN:
        specs.append(
            pl.BlockSpec((None, depth, tile), lambda j: (stream, 0, start // tile + j))
        )
    else:
        specs.append(pl.BlockSpec((None, tile, size), lambda j: (stream, j, start // size)))
    for array in extra:
        if array.ndim == 3:
            specs.append(pl.BlockSpec((None, 1, tile), lambda j: (stream, 0, j)))
        else:
            specs.append(pl.BlockSpec((array.shape[0], tile), lambda j: (0, j)))
    count = len(pieces)

    def kernel(*refs):
        extras, results = refs[count + 1 : count + 1 + len(extra)], refs[count + 1 + len(extra) :]
        at = 0
        for n, (unused, rows, which) in enumerate(pieces):
            product = dot(refs[n][...], refs[count][...], dims)
            epilogue(n, slice(at, at + rows), product, extras, results)
            at += rows

    return pl.pallas_call(
        kernel,
        grid=(columns // tile,),
        in_specs=specs,
        out_specs=[pl.BlockSpec((rows, tile), lambda j: (0, j)) for rows, unused in outs],
        out_shape=[jax.ShapeDtypeStruct((rows, columns), kind) for rows, kind in outs],
        compiler_params=VMEM,
        cost_estimate=COST,
        name=name,
    )(*[piece[0] for piece in pieces], weights, *extra)


def low_of(n, rows, product, extras, results):
    results[0][rows] = product.astype(BF16)


def low_biased(n, rows, product, extras, results):
    results[0][rows] = (product + extras[0][...]).astype(BF16)


def gelu_biased(n, rows, product, extras, results):
    value, slope = gelu_pair(product + extras[0][...])
    results[0][rows] = value.astype(BF16)
    results[1][rows] = slope


def sloped(n, rows, product, extras, results):
    low = (product * extras[0][rows]).astype(BF16)
    results[0][rows] = low
    total = column_sum(low.astype(F32))
    results[1][...] = total if n == 0 else results[1][...] + total


def apart(n, rows, product, extras, results):
    results[n][...] = product.astype(results[n].dtype)


def ring_of(chips):
    wide = 1
    while (2 * wide) ** 2 <= chips:
        wide *= 2
    long = chips // wide
    order = [row * wide for row in range(long)]
    for turn, row in enumerate(reversed(range(long))):
        across = list(range(1, wide))
        order += [row * wide + col for col in (across if turn % 2 == 0 else across[::-1])]
    return order


class Rings:
    def __init__(self, dp, kind=BF16):
        self.kind, self.dp = kind, dp
        self.chips = dp // 2
        order = ring_of(self.chips)
        me = lax.axis_index("dp")
        chip, self.core = me // 2, me % 2
        self.hops, self.targets = [], []
        for way in (1, -1):
            self.hops.append(
                [
                    (2 * order[i] + c, 2 * order[(i + way) % self.chips] + c)
                    for i in range(self.chips)
                    for c in range(2)
                ]
            )
            targets = []
            for step in range(self.chips):
                at = jnp.int32(0)
                for spot, here in enumerate(order):
                    goal = order[(spot - way * (1 + step)) % self.chips]
                    at = at + jnp.where(chip == here, goal, 0)
                targets.append(at)
            self.targets.append(targets)
        self.views, self.flying = ([], []), ([], [])
        self.step = 0
        self.result = None

    def give(self, stream, keep, gift):
        self.views[stream].append(keep)
        swap = [(i, i ^ 1) for i in range(self.dp)]
        self.flying[stream].append(lax.ppermute(gift, "dp", swap))

    def add(self, came):
        last = self.step == self.chips - 1
        widths = [view.shape[-1] for view in self.views[0]]
        rows = self.views[0][0].shape[1]
        tile = rows // 2 if rows % 32 == 0 else rows
        at = jnp.stack([self.targets[s][self.step] for s in range(2)])
        operands, specs, places = [], [], []
        for s in range(2):
            for view, got in zip(self.views[s], self.got[s]):
                width = view.shape[-1]
                operands += [view, got]
                block = pl.BlockSpec((None, tile, width), lambda i, at, s=s: (at[s], i, 0))
                specs += [block, block]
            if came is not None:
                operands.append(came[s])
                specs.append(pl.BlockSpec((tile, sum(widths)), lambda i, at: (i, 0)))
        sizes = widths if last else [sum(widths)]
        kind = F32 if last else self.kind
        shapes = [jax.ShapeDtypeStruct((rows, size), kind) for size in sizes] * 2

        def kernel(at_ref, *refs):
            ins, outs = refs[: len(operands)], refs[len(operands) :]
            per_way = len(operands) // 2
            for s in range(2):
                mine = ins[s * per_way : (s + 1) * per_way]
                start = 0
                for number, width in enumerate(widths):
                    value = mine[2 * number][...].astype(F32) + mine[2 * number + 1][...].astype(F32)
                    if came is not None:
                        value = value + mine[-1][:, start : start + width].astype(F32)
                    if last:
                        outs[s * len(sizes) + number][...] = value
                    else:
                        outs[s][:, start : start + width] = value.astype(kind)
                    start += width

        out = pl.pallas_call(
            kernel,
            grid_spec=pltpu.PrefetchScalarGridSpec(
                num_scalar_prefetch=1,
                grid=(rows // tile,),
                in_specs=specs,
                out_specs=[
                    pl.BlockSpec((tile, shape.shape[1]), lambda i, at: (i, 0)) for shape in shapes
                ],
            ),
            out_shape=shapes,
            compiler_params=VMEM,
            cost_estimate=COST,
            name="ring_add",
        )(at, *operands)
        return [out[s * len(sizes) : (s + 1) * len(sizes)] for s in range(2)]

    def advance(self):
        if self.step == 0:
            self.got = self.flying
            total = self.add(None)
        else:
            total = self.add([flight[0] for flight in self.flying])
        self.sent = total
        if self.step == self.chips - 1:
            self.result = total
            self.flying = ([], [])
        else:
            self.flying = tuple(
                [lax.ppermute(total[s][0], "dp", self.hops[s])] for s in range(2)
            )
        self.step += 1

    def finish(self):
        while self.result is None:
            self.advance()
        return self.result


def beat(value, rings):
    if rings.result is None:
        value, rings.flying = lax.optimization_barrier((value, rings.flying))
        rings.advance()
        value, unused = lax.optimization_barrier((value, rings.sent))
    return value


def tie(*values):
    return lax.optimization_barrier(values)


def body(
    mp,
    dp,
    image_tokens,
    text_tokens,
    condition,
    live_table,
    ada_weight,
    ada_bias,
    qkv_weight,
    qv_bias,
    proj_weight,
    proj_bias,
    fc1_weight,
    fc1_bias,
    fc2_weight,
    fc2_bias,
    image_cotangent,
    text_cotangent,
):
    seqs, width = image_tokens.shape[0], image_tokens.shape[2]
    my_dp = lax.axis_index("dp")
    swap = [(0, 1), (1, 0)]

    def share(rows):
        if mp == 2:
            return whole(flat(rows)) + whole(flat(lax.ppermute(rows, "mp", swap)))
        return whole(flat(lax.all_gather(rows, "mp", axis=0, tiled=False)))

    def split(array):
        return halves(array, 2 if mp == 2 else 1)

    def collect(array, weights, stream, start, size, name):
        pieces = split(array)
        outs = [(piece[1], kind) for piece, kind in zip(pieces, (F32, BF16))]
        parts = matmul(pieces, weights, stream, NT, start, size, apart, outs, [], name)
        if mp == 2:
            shape = (1, seqs, -1, width)
            return [parts[0].reshape(shape), parts[1].reshape(shape[1:])]

        low = parts[0].astype(BF16).reshape(mp, seqs, -1, width)
        return [low, low[0]]

    def exchange(parts):
        if mp == 2:
            return parts[0], lax.ppermute(parts[1], "mp", swap)
        low = lax.psum_scatter(parts[0], "mp", scatter_dimension=0, tiled=False)
        return low.astype(F32), jnp.zeros_like(low)

    def sum_mp(values):
        if mp == 2:
            return values + lax.ppermute(values, "mp", swap)
        return lax.psum(values, "mp")

    def flat(array):
        return array.reshape(-1, array.shape[-1])

    def gather_small(rows, after=lambda rows: rows):
        shape, reach, bits = rows.shape, dp // 2, 0
        while reach >= 1:
            other = lax.ppermute(rows, "dp", [(i, i ^ reach) for i in range(dp)])
            low_half = (my_dp & reach) == 0
            rows = jnp.concatenate(
                [jnp.where(low_half, rows, other), jnp.where(low_half, other, rows)], axis=0
            )
            rows = after(rows)
            reach, bits = reach // 2, bits + 1
        rows = rows.reshape((2,) * bits + shape)
        order = tuple(reversed(range(bits))) + tuple(range(bits, bits + len(shape)))
        return rows.transpose(order).reshape((dp,) + shape)

    small = [condition, ada_bias, qv_bias, proj_bias, fc1_bias, fc2_bias]
    sizes = [a.size for a in small]
    packed = jnp.concatenate([a.astype(BF16).reshape(-1) for a in small])
    packed = jnp.pad(packed, (0, -packed.size % 2048)).reshape(-1, 128)
    packed = gather_small(packed).reshape(dp, -1)
    pieces, at = [], 0
    for array, size in zip(small, sizes):
        pieces.append(packed[:, at : at + size].reshape((dp,) + array.shape))
        at += size
    cond_all = pieces[0].reshape(dp * seqs, -1)
    ada_biases, proj_biases, up_biases, down_biases = (
        jnp.moveaxis(pieces[i], 0, 1).reshape(2, -1).astype(F32) for i in (1, 3, 4, 5)
    )
    qv_biases = jnp.moveaxis(pieces[2], 0, 2).reshape(2, 2, -1).astype(F32)

    share_rows, heads_width = qkv_weight.shape[2:]
    lanes = head_block(heads_width)
    qkv_low = qkv_weight.astype(BF16).reshape(2, 3, share_rows, -1, lanes)
    qkv_low = qkv_low.transpose(0, 2, 3, 1, 4).reshape(2, share_rows, -1)
    proj_low = jnp.swapaxes(proj_weight.astype(BF16), 1, 2)
    attention_full = lax.all_gather(
        jnp.concatenate([qkv_low, proj_low], axis=2), "dp", axis=1, tiled=True
    )
    qkv_size = 3 * heads_width
    up_full = lax.all_gather(fc1_weight.astype(BF16), "dp", axis=1, tiled=True)
    down_full = lax.all_gather(
        jnp.swapaxes(fc2_weight.astype(BF16), 1, 2), "dp", axis=1, tiled=True
    )
    biases = qv_biases.reshape(2, 2, -1, lanes)
    biases = jnp.stack([biases[:, 0], jnp.zeros_like(biases[:, 0]), biases[:, 1]], axis=2)
    biases = biases.reshape(2, 1, -1)

    ada_low = ada_weight.astype(BF16)
    ada_rows = ada_low.shape[1]
    silu_all = jax.nn.silu(cond_all.astype(F32)).astype(BF16)
    silu_mine = lax.dynamic_slice_in_dim(silu_all, my_dp * ada_rows, ada_rows, axis=1)
    core = lax.rem(my_dp, 2)
    mod_rings = Rings(dp, F32)
    for s in range(2):
        partial = dot(silu_mine, ada_low[s], NN).reshape(dp // 2, 2, -1, 128)
        keep, gift = (lax.dynamic_index_in_dim(partial, c, 1, False) for c in (core, 1 - core))
        mod_rings.give(s, keep, gift)
    modulation = jnp.stack([part[0].reshape(seqs, -1) for part in mod_rings.finish()], axis=1)
    modulation = (sum_mp(modulation) + ada_biases).reshape(seqs, 2, 6, width)
    mod = [modulation[:, s] for s in range(2)]
    live = live_table[0]
    tokens, cotangents = (image_tokens, text_tokens), (image_cotangent, text_cotangent)
    rows_of = [t.shape[1] for t in tokens]

    joint_in, branch_low, branch_sum = [], [], []
    for s in range(2):
        low, branch, total = stage(
            enter_kernel,
            live,
            [tokens[s], cotangents[s], mod[s]],
            [rows_of[s], rows_of[s], 1],
            [BF16, BF16, F32],
            "enter",
        )
        joint_in.append(share(low))
        branch_low.append(branch)
        branch_sum.append(total)
    branch_low, joint_in = tie(branch_low, [[piece[0] for piece in pieces] for pieces in joint_in])
    joint_in = [[piece for array in arrays for piece in whole(array)] for arrays in joint_in]
    down_up = [share(branch_low[s]) for s in range(2)]
    all_rows = [mp * seqs * rows_of[s] for s in range(2)]
    units = up_biases.shape[1]

    qkv = []
    for s in range(2):
        (product,) = matmul(
            joint_in[s],
            attention_full,
            s,
            NN,
            0,
            qkv_size,
            low_biased,
            [(all_rows[s], BF16)],
            [biases],
            "qkv",
        )
        qkv.append(product.reshape(mp, seqs, rows_of[s], -1))
    attended, arrived = tie(
        attention_forward(qkv[0], qkv[1]), [[piece[0] for piece in pieces] for pieces in down_up]
    )
    attended = [flat(o) for o in attended]
    down_up = [[piece for array in arrays for piece in whole(array)] for arrays in arrived]

    residual, first_branch, mlp_in = [None, None], [None, None], [None, None]
    sums = []
    for s in range(2):
        parts = collect(attended[s], attention_full, s, qkv_size, heads_width, "proj")
        sums.append(exchange(parts))
    for s in (1, 0):
        first_branch[s], residual[s], low = stage(
            middle_kernel,
            live,
            [*sums[s], tokens[s], proj_biases[s : s + 1], mod[s]],
            [rows_of[s]] * 3,
            [F32, F32, BF16],
            "middle",
        )
        mlp_in[s] = share(low)

    slope, active = [None, None], [None, None]
    rings, last_rings = Rings(dp), Rings(dp)
    up_bias_rows = up_biases.reshape(2, 1, -1)
    for s in (1, 0):
        active[s], slope[s] = matmul(
            mlp_in[s],
            up_full,
            s,
            NN,
            0,
            units,
            gelu_biased,
            [(all_rows[s], BF16), (all_rows[s], F32)],
            [up_bias_rows],
            "up",
        )
        keep, gift = weight_grad(down_up[s], split(active[s]), core, dp)
        keep, gift, slope = tie(keep, gift, slope)
        rings.give(s, keep, gift)

    grad_pre, back, up_sums = [], [], []
    for s in range(2):
        low, total = matmul(
            down_up[s],
            down_full,
            s,
            NN,
            0,
            units,
            sloped,
            [(all_rows[s], BF16), (1, F32)],
            [slope[s]],
            "down_back",
        )
        grad_pre.append(low)
        up_sums.append(total)
        back.append(collect(low, up_full, s, 0, units, "up_back"))
        back[s], slope, grad_pre = tie(back[s], slope, grad_pre)
        back[s] = exchange(back[s])
    keep, gift = weight_grad(mlp_in[0], split(grad_pre[0]), core, dp)
    keep, gift, grad_pre, back[0] = tie(keep, gift, grad_pre, back[0])
    rings.give(0, keep, gift)
    keep, gift = weight_grad(mlp_in[1], split(grad_pre[1]), core, dp)
    keep, gift, back[1] = tie(keep, gift, back[1])
    rings.give(1, keep, gift)
    back = beat(back, rings)
    back, unused = tie(back, rings.sent)

    resid_grad, attention_low, middle_sums, proj_sums = [], [], [], []
    for s in range(2):
        grad, low, total, bias_total = stage(
            middle_back_kernel,
            live,
            [*back[s], cotangents[s], residual[s], first_branch[s], mod[s]],
            [rows_of[s], rows_of[s], 3, 1],
            [F32, BF16, F32, F32],
            "middle_back",
        )
        resid_grad.append(grad)
        attention_low.append(low)
        middle_sums.append(total)
        proj_sums.append(bias_total)
    attention_low, active, middle_sums = tie(attention_low, active, middle_sums)
    attention_low = [share(rows) for rows in attention_low]
    active = beat(active, rings)
    down_sum = [collect(active[s], down_full, s, 0, units, "down") for s in range(2)]
    down_sum, middle_sums = beat((down_sum, middle_sums), rings)

    arrived, down_sum = tie([[piece[0] for piece in pieces] for pieces in attention_low], down_sum)
    attention_low = [[piece for array in arrays for piece in whole(array)] for arrays in arrived]
    down_sum = [exchange(down_sum[s]) for s in range(2)]

    mixed = []
    for s in range(2):
        (product,) = matmul(
            attention_low[s],
            attention_full,
            s,
            NN,
            qkv_size,
            heads_width,
            low_of,
            [(all_rows[s], BF16)],
            [],
            "proj_back",
        )
        mixed.append(product.reshape(mp, seqs, rows_of[s], -1))
    mixed, attended = beat((mixed, attended), rings)
    for s in range(2):
        keep, gift = weight_grad(attention_low[s], split(attended[s]), core, dp)
        keep, gift, mixed, attended = tie(keep, gift, mixed, attended)
        last_rings.give(s, keep, gift)
    grad_qkv = ()
    for n in range(seqs):
        grad_qkv = attention_backward(qkv[0], qkv[1], mixed[0], mixed[1], n, grad_qkv)
        if n == 1:
            grad_qkv, mixed, last_rings.flying, down_sum = tie(
                grad_qkv, mixed, last_rings.flying, down_sum
            )
        else:
            grad_qkv, mixed = beat((grad_qkv, mixed), rings)
    grad_qkv = [flat(g) for g in grad_qkv]

    back = [None, None]
    for s in range(2):
        back[s] = collect(grad_qkv[s], attention_full, s, 0, qkv_size, "qkv_back")
        back[s], grad_qkv = tie(back[s], grad_qkv)
        back[s] = exchange(back[s])
    grad_qkv = beat(grad_qkv, rings)
    for s in range(2):
        keep, gift = weight_grad(joint_in[s], split(grad_qkv[s]), core, dp)
        keep, gift, grad_qkv = tie(keep, gift, grad_qkv)
        last_rings.give(s, keep, gift)
    down_sum, grad_qkv = beat((down_sum, grad_qkv), last_rings)
    outputs, gate_two = [], []
    for s in range(2):
        out, total = stage(
            leave_kernel,
            live,
            [*down_sum[s], residual[s], cotangents[s], down_biases[s : s + 1], mod[s]],
            [rows_of[s], 1],
            [BF16, F32],
            "leave",
        )
        outputs.append(out)
        gate_two.append(total)
    qv_sums = []
    for s in range(2):
        total = jnp.sum(grad_qkv[s].astype(F32), axis=0).reshape(-1, 3, lanes)
        qv_sums += [total[:, 0], total[:, 2]]
    unit_sums = jnp.concatenate([u.reshape(-1) for u in qv_sums + up_sums])
    unit_size = unit_sums.size
    unit_sums = jnp.pad(unit_sums, (0, -unit_size % (seqs * width))).reshape(seqs, -1, width)
    unit_rows = unit_sums.shape[1]
    gate_two, unit_sums = beat((gate_two, unit_sums), last_rings)
    gate_two, unit_sums = beat((gate_two, unit_sums), rings)
    back, gate_two, unit_sums = tie(back, gate_two, unit_sums)

    input_grads, first_sums = [], []
    for s in range(2):
        grad, total = stage(
            enter_back_kernel,
            live,
            [*back[s], tokens[s], resid_grad[s], mod[s]],
            [rows_of[s], 2],
            [F32, F32],
            "enter_back",
        )
        input_grads.append(grad)
        first_sums.append(total)
    packed_sums, picks = [], []
    for s in range(2):
        at = len(packed_sums)
        packed_sums += [first_sums[s], middle_sums[s], gate_two[s]]
        picks += [(at, 0), (at, 1)] + [(at + 1, row) for row in range(3)] + [(at + 2, 0)]
    for array in proj_sums + branch_sum:
        picks.append((len(packed_sums), 0))
        packed_sums.append(array)
    token_rows = len(picks)
    picks += [(len(packed_sums), row) for row in range(unit_rows)]
    sums = pack(packed_sums + [unit_sums], picks, "pack")
    sums, input_grads = beat((sums, input_grads), last_rings)
    if mp == 2:
        other = lax.ppermute(sums, "mp", swap)
        row_of = lax.broadcasted_iota(jnp.int32, sums.shape, 1)
        other = jnp.where(row_of < token_rows, other.astype(F32), 0.0)
        sums = (sums.astype(F32) + other).astype(BF16)
    else:
        sums = jnp.concatenate(
            [lax.psum(sums[:, :token_rows], "mp"), sums[:, token_rows:]], axis=1
        )
    gathered = lax.all_gather(sums, "dp", axis=0, tiled=True)
    input_grads = beat(input_grads, last_rings)
    while rings.result is None:
        input_grads = beat(input_grads, rings)
    input_grads = beat(input_grads, last_rings)
    fc2_out, fc1_out = (jnp.stack([part[n] for part in rings.finish()]) for n in range(2))
    fc2_out = jnp.swapaxes(fc2_out, 1, 2)
    fc1_out, fc2_out = beat((fc1_out, fc2_out), last_rings)
    gathered, unused = tie(gathered, last_rings.sent)

    mod_all = [gathered[:, 6 * s : 6 * s + 6].reshape(dp * seqs, 6 * width) for s in range(2)]
    silu_grad = sum(dot(mod_all[s], ada_low[s], NT) for s in range(2))
    silu_grad = gather_small(silu_grad, lambda rows: beat(rows, last_rings))
    silu_grad, gathered = tie(silu_grad, gathered)
    silu_grad = lax.dynamic_slice_in_dim(silu_grad, my_dp * seqs, seqs, axis=1)
    silu_grad = jnp.moveaxis(silu_grad, 0, 1).reshape(seqs, -1)
    unused, pullback = jax.vjp(jax.nn.silu, condition.astype(F32))
    cond_out = pullback(silu_grad)[0]
    bias_all = jnp.sum(gathered[:, 12:token_rows].astype(F32), axis=0)
    unit_all = jnp.sum(gathered[:, token_rows:].astype(F32).reshape(dp, -1), axis=0)
    qv_size = qv_biases.size

    proj_out, qkv_out = (jnp.stack([part[n] for part in last_rings.finish()]) for n in range(2))
    proj_out = jnp.swapaxes(proj_out, 1, 2)
    qkv_out = qkv_out.reshape(2, share_rows, -1, 3, lanes)
    qkv_out = qkv_out.transpose(0, 3, 1, 2, 4).reshape(qkv_weight.shape)

    def own(total, axis):
        part = total.shape[axis] // dp
        return lax.dynamic_slice_in_dim(total, my_dp * part, part, axis=axis)

    proj_bias_out = own(bias_all[0:2], 1)
    fc2_bias_out = own(bias_all[2:4], 1)
    fc1_bias_out = own(unit_all[qv_size:unit_size].reshape(2, -1), 1)
    qv_bias_out = own(unit_all[:qv_size].reshape(qv_biases.shape), 2)
    ada_bias_out = own(jnp.stack([jnp.sum(m.astype(F32), axis=0) for m in mod_all]), 1)
    ada_out = jnp.stack([dot(silu_mine, mod_all[s], TN) for s in range(2)])

    return (
        outputs[0],
        outputs[1],
        ada_out,
        ada_bias_out,
        qkv_out,
        qv_bias_out,
        proj_out,
        proj_bias_out,
        fc1_out,
        fc1_bias_out,
        fc2_out,
        fc2_bias_out,
        input_grads[0],
        input_grads[1],
        cond_out,
    )


def solution(mesh):
    tokens = P("dp", "mp", None)
    weights = (
        P(None, ("mp", "dp"), None),
        P(None, "dp"),
        P(None, None, "dp", "mp"),
        P(None, None, ("mp", "dp")),
        P(None, "mp", "dp"),
        P(None, "dp"),
        P(None, "dp", "mp"),
        P(None, ("mp", "dp")),
        P(None, "mp", "dp"),
        P(None, "dp"),
    )
    return jax.shard_map(
        functools.partial(body, mesh.shape["mp"], mesh.shape["dp"]),
        mesh=mesh,
        in_specs=(tokens, tokens, P("dp", "mp"), P("dp", None)) + weights + (tokens, tokens),
        out_specs=(tokens, tokens) + weights + (tokens, tokens, P("dp", "mp")),
        check_vma=False,
    )
```

```python
import functools

import jax
import jax.numpy as jnp
from jax import lax
from jax.experimental import pallas as pl
from jax.experimental.pallas import tpu as pltpu
from jax.sharding import PartitionSpec as P

HEAD_DIM = 64
EPSILON = 1e-06
F32 = jnp.float32
BF16 = jnp.bfloat16


def gelu_pair(values):
    root, cubic = (2.0 / 3.141592653589793) ** 0.5, 0.044715
    square = values * values
    bend = jnp.tanh(root * values * (1.0 + cubic * square))
    half = 0.5 * (1.0 + bend)
    slope = half + 0.5 * values * (1.0 - bend * bend) * root * (1.0 + 3.0 * cubic * square)
    return values * half, slope


def dot(left, right, dims):
    return lax.dot_general(left, right, (dims, ((), ())), preferred_element_type=F32)


NN = ((1,), (0,))
NT = ((1,), (1,))
TN = ((0,), (0,))


def join_rows(text_ref, image_ref):
    width = text_ref.shape[-1]
    return jnp.concatenate(
        [text_ref[...].reshape(-1, width), image_ref[...].reshape(-1, width)], axis=0
    )


def parts_of(joined):
    lanes = joined.shape[1] // 3
    return [joined[:, place * lanes : (place + 1) * lanes] for place in range(3)]


def attention_kernel(image_ref, text_ref, oi, ot):
    query, key, value = parts_of(join_rows(text_ref, image_ref))
    width = query.shape[1]
    head_of = lax.broadcasted_iota(jnp.int32, query.shape, 1) // HEAD_DIM
    out = jnp.zeros(query.shape, F32)
    for head in range(width // HEAD_DIM):
        inside = head_of == head
        scores = dot(jnp.where(inside, query, jnp.zeros_like(query)), key, NT) * HEAD_DIM**-0.5
        raised = jnp.exp(scores - jnp.max(scores, axis=1, keepdims=True))
        probs = raised * (1.0 / jnp.sum(raised, axis=1, keepdims=True))
        out = jnp.where(inside, dot(probs.astype(BF16), value, NN), out)
    text_rows = ot.shape[0] * ot.shape[1]
    ot[...] = out[:text_rows].astype(BF16).reshape(ot.shape)
    oi[...] = out[text_rows:].astype(BF16).reshape(oi.shape)


def attention_back_kernel(image_ref, text_ref, gi, gt, di, dt):
    query, key, value = parts_of(join_rows(text_ref, image_ref))
    grad = join_rows(gt, gi)
    width = query.shape[1]
    head_of = lax.broadcasted_iota(jnp.int32, query.shape, 1) // HEAD_DIM
    blank = jnp.zeros_like(query)
    dq, dk, dv = (jnp.zeros(query.shape, F32) for _ in range(3))
    scale = HEAD_DIM**-0.5
    for head in range(width // HEAD_DIM):
        inside = head_of == head
        scores = dot(jnp.where(inside, key, blank), query, NT) * scale
        raised = jnp.exp(scores - jnp.max(scores, axis=0, keepdims=True))
        probs = raised * (1.0 / jnp.sum(raised, axis=0, keepdims=True))
        grad_probs = dot(jnp.where(inside, value, blank), grad, NT)
        delta = jnp.sum(probs * grad_probs, axis=0, keepdims=True)
        grad_scores = (probs * (grad_probs - delta)).astype(BF16)
        dv = jnp.where(inside, dot(probs.astype(BF16), grad, NN), dv)
        dk = jnp.where(inside, dot(grad_scores, query, NN) * scale, dk)
        dq = jnp.where(inside, dot(grad_scores, key, TN) * scale, dq)
    text_rows = dt.shape[0] * dt.shape[1]
    low = jnp.concatenate([part.astype(BF16) for part in (dq, dk, dv)], axis=1)
    dt[...] = low[:text_rows].reshape(dt.shape)
    di[...] = low[text_rows:].reshape(di.shape)


def head_block(width):
    return 128 if width % 128 == 0 else width


def blocked(shape, lanes, first=0):
    return pl.BlockSpec(
        (shape[0], None, shape[2], lanes), lambda seq, block: (0, seq + first, 0, block)
    )


VMEM = pltpu.CompilerParams(vmem_limit_bytes=48 * 2**20)
COST = pl.CostEstimate(flops=1024, transcendentals=0, bytes_accessed=1024)


def attention_forward(image, text):
    seqs, width = image.shape[1], image.shape[3] // 3
    lanes = head_block(width)
    shapes = [jax.ShapeDtypeStruct(a.shape[:3] + (width,), BF16) for a in (image, text)]
    return pl.pallas_call(
        attention_kernel,
        grid=(seqs, width // lanes),
        in_specs=[blocked(a.shape, 3 * lanes) for a in (image, text)],
        out_specs=[blocked(s.shape, lanes) for s in shapes],
        out_shape=shapes,
        compiler_params=VMEM,
        cost_estimate=COST,
        name="attention_forward",
    )(image, text)


def attention_backward(image, text, image_grad, text_grad, first, into):
    width = image.shape[3] // 3
    lanes = head_block(width)
    specs = [blocked(a.shape, 3 * lanes, first) for a in (image, text)]
    specs += [blocked(a.shape, lanes, first) for a in (image_grad, text_grad)]
    kernel = attention_back_kernel
    if into:
        specs += [pl.BlockSpec(memory_space=pl.ANY)] * 2

        def kernel(image_ref, text_ref, gi, gt, unused_image, unused_text, di, dt):
            attention_back_kernel(image_ref, text_ref, gi, gt, di, dt)

    return pl.pallas_call(
        kernel,
        grid=(1, width // lanes),
        in_specs=specs,
        out_specs=[blocked(a.shape, 3 * lanes, first) for a in (image, text)],
        out_shape=[jax.ShapeDtypeStruct(a.shape, BF16) for a in (image, text)],
        input_output_aliases={4: 0, 5: 1} if into else {},
        compiler_params=VMEM,
        cost_estimate=COST,
        name="attention_backward",
    )(image, text, image_grad, text_grad, *into)


def centred(values):
    center = values - jnp.mean(values, axis=-1, keepdims=True)
    inverse = lax.rsqrt(jnp.mean(center * center, axis=-1, keepdims=True) + EPSILON)
    return center * inverse, inverse


def norm_back(normed, inverse, upstream):
    mean_up = jnp.mean(upstream, axis=-1, keepdims=True)
    mean_cross = jnp.mean(upstream * normed, axis=-1, keepdims=True)
    return inverse * (upstream - mean_up - normed * mean_cross)


def column_sum(values):
    return jnp.sum(values, axis=0, keepdims=True)


def enter_kernel(live_ref, tokens, cot, mod, low_ref, branch_ref, sum_ref):
    live = live_ref[pl.program_id(0)].astype(F32)
    normed, unused = centred(tokens[...].astype(F32))
    low_ref[...] = (normed * (1.0 + mod[1:2]) + mod[0:1]).astype(BF16)
    branch = cot[...].astype(F32) * live * mod[5:6]
    branch_ref[...] = branch.astype(BF16)
    sum_ref[...] = column_sum(branch)


def middle_kernel(live_ref, kept, came, tokens, bias, mod, branch_ref, resid_ref, low_ref):
    branch = kept[...] + came[...].astype(F32) + bias[...]
    resid = tokens[...].astype(F32) + mod[2:3] * branch
    normed, unused = centred(resid)
    branch_ref[...] = branch
    resid_ref[...] = resid
    low_ref[...] = (normed * (1.0 + mod[4:5]) + mod[3:4]).astype(BF16)


def middle_back_kernel(
    live_ref, kept, came, cot, resid, branch, mod, grad_ref, low_ref, sum_ref, bias_ref
):
    live = live_ref[pl.program_id(0)].astype(F32)
    back = kept[...] + came[...].astype(F32)
    normed, inverse = centred(resid[...])
    grad = cot[...].astype(F32) * live + norm_back(normed, inverse, back * (1.0 + mod[4:5]))
    grad_ref[...] = grad
    low = grad * mod[2:3]
    low_ref[...] = low.astype(BF16)
    sum_ref[0:1] = column_sum(grad * branch[...])
    sum_ref[1:2] = column_sum(back)
    sum_ref[2:3] = column_sum(back * normed)
    bias_ref[...] = column_sum(low)


def leave_kernel(live_ref, kept, came, resid, cot, bias, mod, out_ref, sum_ref):
    live = live_ref[pl.program_id(0)].astype(F32)
    branch = kept[...] + came[...].astype(F32) + bias[...]
    out_ref[...] = (live * (resid[...] + mod[5:6] * branch)).astype(BF16)
    sum_ref[...] = column_sum(cot[...].astype(F32) * live * branch)


def enter_back_kernel(live_ref, kept, came, tokens, grad, mod, grad_ref, sum_ref):
    back = kept[...] + came[...].astype(F32)
    normed, inverse = centred(tokens[...].astype(F32))
    grad_ref[...] = grad[...] + norm_back(normed, inverse, back * (1.0 + mod[1:2]))
    sum_ref[0:1] = column_sum(back)
    sum_ref[1:2] = column_sum(back * normed)


def stage(kernel, live, arrays, rows, kinds, name):
    seqs, width = live.shape[0], arrays[0].shape[-1]
    specs = []
    for array in arrays:
        if array.ndim == 2:
            specs.append(pl.BlockSpec((1, width), lambda i, live_ref: (0, 0)))
        elif array.ndim == 3:
            block = (None,) + array.shape[1:]
            specs.append(pl.BlockSpec(block, lambda i, live_ref: (i, 0, 0)))
        else:
            block = (None, None) + array.shape[2:]
            specs.append(pl.BlockSpec(block, lambda i, live_ref: (0, i, 0, 0)))
    shapes = [jax.ShapeDtypeStruct((seqs, r, width), kind) for r, kind in zip(rows, kinds)]
    return pl.pallas_call(
        kernel,
        grid_spec=pltpu.PrefetchScalarGridSpec(
            num_scalar_prefetch=1,
            grid=(seqs,),
            in_specs=specs,
            out_specs=[
                pl.BlockSpec((None, r, width), lambda i, live_ref: (i, 0, 0)) for r in rows
            ],
        ),
        out_shape=shapes,
        compiler_params=VMEM,
        cost_estimate=COST,
        name=name,
    )(live, *arrays)


def pack(arrays, picks, name):
    seqs, width = arrays[0].shape[0], arrays[0].shape[2]

    def kernel(*refs):
        refs[-1][...] = jnp.concatenate(
            [refs[array][row : row + 1] for array, row in picks], axis=0
        ).astype(BF16)

    return pl.pallas_call(
        kernel,
        grid=(seqs,),
        in_specs=[pl.BlockSpec((None,) + a.shape[1:], lambda i: (i, 0, 0)) for a in arrays],
        out_specs=pl.BlockSpec((None, len(picks), width), lambda i: (i, 0, 0)),
        out_shape=jax.ShapeDtypeStruct((seqs, len(picks), width), BF16),
        compiler_params=VMEM,
        cost_estimate=COST,
        name=name,
    )(*arrays)


def whole(array):
    return [(array, array.shape[0], 0)]


def halves(array, count):
    return [(array, array.shape[0] // count, n) for n in range(count)]


def weight_grad(left, right, core, dp):
    width, columns = left[0][0].shape[1], right[0][0].shape[1]
    rows = width // dp
    chips = max(1, 384 // (2 * rows))
    block = chips * 2 * rows
    count = len(left)

    def kernel(core_ref, *refs):
        keep_ref, give_ref = refs[2 * count :]
        value = dot(refs[0][...], refs[count][...], TN)
        for n in range(1, count):
            value = value + dot(refs[n][...], refs[count + n][...], TN)
        value = value.astype(BF16).reshape(chips, 2, rows, columns)
        first = core_ref[0] == 0

        @pl.when(first)
        def unused_first():
            keep_ref[...] = value[:, 0]
            give_ref[...] = value[:, 1]

        @pl.when(jnp.logical_not(first))
        def unused_second():
            keep_ref[...] = value[:, 1]
            give_ref[...] = value[:, 0]

    specs = [
        pl.BlockSpec((depth, block), lambda i, core_ref, which=which: (which, i))
        for unused, depth, which in left
    ]
    specs += [
        pl.BlockSpec(
            (depth, columns),
            lambda i, core_ref, which=which: (which, 0),
            pipeline_mode=pl.Buffered(1),
        )
        for unused, depth, which in right
    ]
    out = pl.BlockSpec((chips, rows, columns), lambda i, core_ref: (i, 0, 0))
    return pl.pallas_call(
        kernel,
        grid_spec=pltpu.PrefetchScalarGridSpec(
            num_scalar_prefetch=1, grid=(width // block,), in_specs=specs, out_specs=[out, out]
        ),
        out_shape=[jax.ShapeDtypeStruct((dp // 2, rows, columns), BF16)] * 2,
        compiler_params=VMEM,
        cost_estimate=COST,
        name="weight_grad",
    )(core.reshape(1), *[piece[0] for piece in left + right])


def matmul(pieces, weights, stream, dims, start, size, epilogue, outs, extra, name):
    if start % 128 or size % 128:
        weights, start = weights[:, :, start : start + size], 0
    depth = weights.shape[1]
    columns = size if dims == NN else depth
    tile = next((t for t in (512, 384) if columns % t == 0), columns)
    specs = [
        pl.BlockSpec(
            (rows, array.shape[1]),
            lambda j, which=which: (which, 0),
            pipeline_mode=pl.Buffered(1),
        )
        for array, rows, which in pieces
    ]
    if dims == NN:
        specs.append(
            pl.BlockSpec((None, depth, tile), lambda j: (stream, 0, start // tile + j))
        )
    else:
        specs.append(pl.BlockSpec((None, tile, size), lambda j: (stream, j, start // size)))
    for array in extra:
        if array.ndim == 3:
            specs.append(pl.BlockSpec((None, 1, tile), lambda j: (stream, 0, j)))
        else:
            specs.append(pl.BlockSpec((array.shape[0], tile), lambda j: (0, j)))
    count = len(pieces)

    def kernel(*refs):
        extras, results = refs[count + 1 : count + 1 + len(extra)], refs[count + 1 + len(extra) :]
        at = 0
        for n, (unused, rows, which) in enumerate(pieces):
            product = dot(refs[n][...], refs[count][...], dims)
            epilogue(n, slice(at, at + rows), product, extras, results)
            at += rows

    return pl.pallas_call(
        kernel,
        grid=(columns // tile,),
        in_specs=specs,
        out_specs=[pl.BlockSpec((rows, tile), lambda j: (0, j)) for rows, unused in outs],
        out_shape=[jax.ShapeDtypeStruct((rows, columns), kind) for rows, kind in outs],
        compiler_params=VMEM,
        cost_estimate=COST,
        name=name,
    )(*[piece[0] for piece in pieces], weights, *extra)


def low_of(n, rows, product, extras, results):
    results[0][rows] = product.astype(BF16)


def low_biased(n, rows, product, extras, results):
    results[0][rows] = (product + extras[0][...]).astype(BF16)


def gelu_biased(n, rows, product, extras, results):
    value, slope = gelu_pair(product + extras[0][...])
    results[0][rows] = value.astype(BF16)
    results[1][rows] = slope


def sloped(n, rows, product, extras, results):
    low = (product * extras[0][rows]).astype(BF16)
    results[0][rows] = low
    total = column_sum(low.astype(F32))
    results[1][...] = total if n == 0 else results[1][...] + total


def apart(n, rows, product, extras, results):
    results[n][...] = product.astype(results[n].dtype)


def ring_of(chips):
    wide = 1
    while (2 * wide) ** 2 <= chips:
        wide *= 2
    long = chips // wide
    order = [row * wide for row in range(long)]
    for turn, row in enumerate(reversed(range(long))):
        across = list(range(1, wide))
        order += [row * wide + col for col in (across if turn % 2 == 0 else across[::-1])]
    return order


class Rings:
    def __init__(self, dp, kind=BF16):
        self.kind, self.dp = kind, dp
        self.chips = dp // 2
        order = ring_of(self.chips)
        me = lax.axis_index("dp")
        chip, self.core = me // 2, me % 2
        self.hops, self.targets = [], []
        for way in (1, -1):
            self.hops.append(
                [
                    (2 * order[i] + c, 2 * order[(i + way) % self.chips] + c)
                    for i in range(self.chips)
                    for c in range(2)
                ]
            )
            targets = []
            for step in range(self.chips):
                at = jnp.int32(0)
                for spot, here in enumerate(order):
                    goal = order[(spot - way * (1 + step)) % self.chips]
                    at = at + jnp.where(chip == here, goal, 0)
                targets.append(at)
            self.targets.append(targets)
        self.views, self.flying = ([], []), ([], [])
        self.step = 0
        self.result = None

    def give(self, stream, keep, gift):
        self.views[stream].append(keep)
        swap = [(i, i ^ 1) for i in range(self.dp)]
        self.flying[stream].append(lax.ppermute(gift, "dp", swap))

    def add(self, came):
        last = self.step == self.chips - 1
        widths = [view.shape[-1] for view in self.views[0]]
        rows = self.views[0][0].shape[1]
        tile = rows // 2 if rows % 32 == 0 and sum(widths) > 4096 else rows
        at = jnp.stack([self.targets[s][self.step] for s in range(2)])
        operands, specs, places = [], [], []
        for s in range(2):
            for view, got in zip(self.views[s], self.got[s]):
                width = view.shape[-1]
                operands += [view, got]
                block = pl.BlockSpec((None, tile, width), lambda i, at, s=s: (at[s], i, 0))
                specs += [block, block]
            if came is not None:
                operands.append(came[s])
                specs.append(pl.BlockSpec((tile, sum(widths)), lambda i, at: (i, 0)))
        sizes = widths if last else [sum(widths)]
        kind = F32 if last else self.kind
        shapes = [jax.ShapeDtypeStruct((rows, size), kind) for size in sizes] * 2

        def kernel(at_ref, *refs):
            ins, outs = refs[: len(operands)], refs[len(operands) :]
            per_way = len(operands) // 2
            for s in range(2):
                mine = ins[s * per_way : (s + 1) * per_way]
                start = 0
                for number, width in enumerate(widths):
                    value = mine[2 * number][...].astype(F32) + mine[2 * number + 1][...].astype(F32)
                    if came is not None:
                        value = value + mine[-1][:, start : start + width].astype(F32)
                    if last:
                        outs[s * len(sizes) + number][...] = value
                    else:
                        outs[s][:, start : start + width] = value.astype(kind)
                    start += width

        out = pl.pallas_call(
            kernel,
            grid_spec=pltpu.PrefetchScalarGridSpec(
                num_scalar_prefetch=1,
                grid=(rows // tile,),
                in_specs=specs,
                out_specs=[
                    pl.BlockSpec((tile, shape.shape[1]), lambda i, at: (i, 0)) for shape in shapes
                ],
            ),
            out_shape=shapes,
            compiler_params=VMEM,
            cost_estimate=COST,
            name="ring_add",
        )(at, *operands)
        return [out[s * len(sizes) : (s + 1) * len(sizes)] for s in range(2)]

    def advance(self):
        if self.step == 0:
            self.got = self.flying
            total = self.add(None)
        else:
            total = self.add([flight[0] for flight in self.flying])
        self.sent = total
        if self.step == self.chips - 1:
            self.result = total
            self.flying = ([], [])
        else:
            self.flying = tuple(
                [lax.ppermute(total[s][0], "dp", self.hops[s])] for s in range(2)
            )
        self.step += 1

    def finish(self):
        while self.result is None:
            self.advance()
        return self.result


def beat(value, rings):
    if rings.result is None:
        value, rings.flying = lax.optimization_barrier((value, rings.flying))
        rings.advance()
        value, unused = lax.optimization_barrier((value, rings.sent))
    return value


def tie(*values):
    return lax.optimization_barrier(values)


def body(
    mp,
    dp,
    image_tokens,
    text_tokens,
    condition,
    live_table,
    ada_weight,
    ada_bias,
    qkv_weight,
    qv_bias,
    proj_weight,
    proj_bias,
    fc1_weight,
    fc1_bias,
    fc2_weight,
    fc2_bias,
    image_cotangent,
    text_cotangent,
):
    seqs, width = image_tokens.shape[0], image_tokens.shape[2]
    my_dp = lax.axis_index("dp")
    swap = [(0, 1), (1, 0)]

    def share(rows):
        if mp == 2:
            return whole(flat(rows)) + whole(flat(lax.ppermute(rows, "mp", swap)))
        return whole(flat(lax.all_gather(rows, "mp", axis=0, tiled=False)))

    def split(array):
        return halves(array, 2 if mp == 2 else 1)

    def collect(array, weights, stream, start, size, name):
        pieces = split(array)
        outs = [(piece[1], kind) for piece, kind in zip(pieces, (F32, BF16))]
        parts = matmul(pieces, weights, stream, NT, start, size, apart, outs, [], name)
        if mp == 2:
            shape = (1, seqs, -1, width)
            return [parts[0].reshape(shape), parts[1].reshape(shape[1:])]

        low = parts[0].astype(BF16).reshape(mp, seqs, -1, width)
        return [low, low[0]]

    def exchange(parts):
        if mp == 2:
            return parts[0], lax.ppermute(parts[1], "mp", swap)
        low = lax.psum_scatter(parts[0], "mp", scatter_dimension=0, tiled=False)
        return low.astype(F32), jnp.zeros_like(low)

    def sum_mp(values):
        if mp == 2:
            return values + lax.ppermute(values, "mp", swap)
        return lax.psum(values, "mp")

    def flat(array):
        return array.reshape(-1, array.shape[-1])

    def gather_small(rows, after=lambda rows: rows):
        shape, reach, bits = rows.shape, dp // 2, 0
        while reach >= 1:
            other = lax.ppermute(rows, "dp", [(i, i ^ reach) for i in range(dp)])
            low_half = (my_dp & reach) == 0
            rows = jnp.concatenate(
                [jnp.where(low_half, rows, other), jnp.where(low_half, other, rows)], axis=0
            )
            rows = after(rows)
            reach, bits = reach // 2, bits + 1
        rows = rows.reshape((2,) * bits + shape)
        order = tuple(reversed(range(bits))) + tuple(range(bits, bits + len(shape)))
        return rows.transpose(order).reshape((dp,) + shape)

    small = [condition, ada_bias, qv_bias, proj_bias, fc1_bias, fc2_bias]
    sizes = [a.size for a in small]
    packed = jnp.concatenate([a.astype(BF16).reshape(-1) for a in small])
    packed = jnp.pad(packed, (0, -packed.size % 2048)).reshape(-1, 128)
    packed = gather_small(packed).reshape(dp, -1)
    pieces, at = [], 0
    for array, size in zip(small, sizes):
        pieces.append(packed[:, at : at + size].reshape((dp,) + array.shape))
        at += size
    cond_all = pieces[0].reshape(dp * seqs, -1)
    ada_biases, proj_biases, up_biases, down_biases = (
        jnp.moveaxis(pieces[i], 0, 1).reshape(2, -1).astype(F32) for i in (1, 3, 4, 5)
    )
    qv_biases = jnp.moveaxis(pieces[2], 0, 2).reshape(2, 2, -1).astype(F32)

    share_rows, heads_width = qkv_weight.shape[2:]
    lanes = head_block(heads_width)
    qkv_low = qkv_weight.astype(BF16).reshape(2, 3, share_rows, -1, lanes)
    qkv_low = qkv_low.transpose(0, 2, 3, 1, 4).reshape(2, share_rows, -1)
    proj_low = jnp.swapaxes(proj_weight.astype(BF16), 1, 2)
    attention_full = lax.all_gather(
        jnp.concatenate([qkv_low, proj_low], axis=2), "dp", axis=1, tiled=True
    )
    qkv_size = 3 * heads_width
    up_full = lax.all_gather(fc1_weight.astype(BF16), "dp", axis=1, tiled=True)
    down_full = lax.all_gather(
        jnp.swapaxes(fc2_weight.astype(BF16), 1, 2), "dp", axis=1, tiled=True
    )
    biases = qv_biases.reshape(2, 2, -1, lanes)
    biases = jnp.stack([biases[:, 0], jnp.zeros_like(biases[:, 0]), biases[:, 1]], axis=2)
    biases = biases.reshape(2, 1, -1)

    ada_low = ada_weight.astype(BF16)
    ada_rows = ada_low.shape[1]
    silu_all = jax.nn.silu(cond_all.astype(F32)).astype(BF16)
    silu_mine = lax.dynamic_slice_in_dim(silu_all, my_dp * ada_rows, ada_rows, axis=1)
    core = lax.rem(my_dp, 2)
    mod_rings = Rings(dp, F32)
    for s in range(2):
        partial = dot(silu_mine, ada_low[s], NN).reshape(dp // 2, 2, -1, 128)
        keep, gift = (lax.dynamic_index_in_dim(partial, c, 1, False) for c in (core, 1 - core))
        mod_rings.give(s, keep, gift)
    modulation = jnp.stack([part[0].reshape(seqs, -1) for part in mod_rings.finish()], axis=1)
    modulation = (sum_mp(modulation) + ada_biases).reshape(seqs, 2, 6, width)
    mod = [modulation[:, s] for s in range(2)]
    live = live_table[0]
    tokens, cotangents = (image_tokens, text_tokens), (image_cotangent, text_cotangent)
    rows_of = [t.shape[1] for t in tokens]

    joint_in, branch_low, branch_sum = [], [], []
    for s in range(2):
        low, branch, total = stage(
            enter_kernel,
            live,
            [tokens[s], cotangents[s], mod[s]],
            [rows_of[s], rows_of[s], 1],
            [BF16, BF16, F32],
            "enter",
        )
        joint_in.append(share(low))
        branch_low.append(branch)
        branch_sum.append(total)
    branch_low, joint_in = tie(branch_low, [[piece[0] for piece in pieces] for pieces in joint_in])
    joint_in = [[piece for array in arrays for piece in whole(array)] for arrays in joint_in]
    down_up = [share(branch_low[s]) for s in range(2)]
    all_rows = [mp * seqs * rows_of[s] for s in range(2)]
    units = up_biases.shape[1]

    qkv = []
    for s in range(2):
        (product,) = matmul(
            joint_in[s],
            attention_full,
            s,
            NN,
            0,
            qkv_size,
            low_biased,
            [(all_rows[s], BF16)],
            [biases],
            "qkv",
        )
        qkv.append(product.reshape(mp, seqs, rows_of[s], -1))
    attended, arrived = tie(
        attention_forward(qkv[0], qkv[1]), [[piece[0] for piece in pieces] for pieces in down_up]
    )
    attended = [flat(o) for o in attended]
    down_up = [[piece for array in arrays for piece in whole(array)] for arrays in arrived]

    residual, first_branch, mlp_in = [None, None], [None, None], [None, None]
    sums = []
    for s in range(2):
        parts = collect(attended[s], attention_full, s, qkv_size, heads_width, "proj")
        sums.append(exchange(parts))
    for s in (1, 0):
        first_branch[s], residual[s], low = stage(
            middle_kernel,
            live,
            [*sums[s], tokens[s], proj_biases[s : s + 1], mod[s]],
            [rows_of[s]] * 3,
            [F32, F32, BF16],
            "middle",
        )
        mlp_in[s] = share(low)

    slope, active = [None, None], [None, None]
    rings, last_rings = Rings(dp), Rings(dp)
    up_bias_rows = up_biases.reshape(2, 1, -1)
    for s in (1, 0):
        active[s], slope[s] = matmul(
            mlp_in[s],
            up_full,
            s,
            NN,
            0,
            units,
            gelu_biased,
            [(all_rows[s], BF16), (all_rows[s], F32)],
            [up_bias_rows],
            "up",
        )
        keep, gift = weight_grad(down_up[s], split(active[s]), core, dp)
        keep, gift, slope = tie(keep, gift, slope)
        rings.give(s, keep, gift)

    grad_pre, back, up_sums = [], [], []
    for s in range(2):
        low, total = matmul(
            down_up[s],
            down_full,
            s,
            NN,
            0,
            units,
            sloped,
            [(all_rows[s], BF16), (1, F32)],
            [slope[s]],
            "down_back",
        )
        grad_pre.append(low)
        up_sums.append(total)
        back.append(collect(low, up_full, s, 0, units, "up_back"))
        back[s], slope, grad_pre = tie(back[s], slope, grad_pre)
        back[s] = exchange(back[s])
    keep, gift = weight_grad(mlp_in[0], split(grad_pre[0]), core, dp)
    keep, gift, grad_pre, back[0] = tie(keep, gift, grad_pre, back[0])
    rings.give(0, keep, gift)
    keep, gift = weight_grad(mlp_in[1], split(grad_pre[1]), core, dp)
    keep, gift, back[1] = tie(keep, gift, back[1])
    rings.give(1, keep, gift)
    back = beat(back, rings)
    back, unused = tie(back, rings.sent)

    resid_grad, attention_low, middle_sums, proj_sums = [], [], [], []
    for s in range(2):
        grad, low, total, bias_total = stage(
            middle_back_kernel,
            live,
            [*back[s], cotangents[s], residual[s], first_branch[s], mod[s]],
            [rows_of[s], rows_of[s], 3, 1],
            [F32, BF16, F32, F32],
            "middle_back",
        )
        resid_grad.append(grad)
        attention_low.append(low)
        middle_sums.append(total)
        proj_sums.append(bias_total)
    attention_low, active, middle_sums = tie(attention_low, active, middle_sums)
    attention_low = [share(rows) for rows in attention_low]
    active = beat(active, rings)
    down_sum = [collect(active[s], down_full, s, 0, units, "down") for s in range(2)]
    down_sum, middle_sums = beat((down_sum, middle_sums), rings)

    arrived, down_sum = tie([[piece[0] for piece in pieces] for pieces in attention_low], down_sum)
    attention_low = [[piece for array in arrays for piece in whole(array)] for arrays in arrived]
    down_sum = [exchange(down_sum[s]) for s in range(2)]

    mixed = []
    for s in range(2):
        (product,) = matmul(
            attention_low[s],
            attention_full,
            s,
            NN,
            qkv_size,
            heads_width,
            low_of,
            [(all_rows[s], BF16)],
            [],
            "proj_back",
        )
        mixed.append(product.reshape(mp, seqs, rows_of[s], -1))
    mixed, attended = beat((mixed, attended), rings)
    for s in range(2):
        keep, gift = weight_grad(attention_low[s], split(attended[s]), core, dp)
        keep, gift, mixed, attended = tie(keep, gift, mixed, attended)
        last_rings.give(s, keep, gift)
    grad_qkv = ()
    for n in range(seqs):
        grad_qkv = attention_backward(qkv[0], qkv[1], mixed[0], mixed[1], n, grad_qkv)
        if n == 1:
            grad_qkv, mixed, last_rings.flying, down_sum = tie(
                grad_qkv, mixed, last_rings.flying, down_sum
            )
        else:
            grad_qkv, mixed = beat((grad_qkv, mixed), rings)
    grad_qkv = [flat(g) for g in grad_qkv]

    back = [None, None]
    for s in range(2):
        back[s] = collect(grad_qkv[s], attention_full, s, 0, qkv_size, "qkv_back")
        back[s], grad_qkv = tie(back[s], grad_qkv)
        back[s] = exchange(back[s])
    grad_qkv = beat(grad_qkv, rings)
    for s in range(2):
        keep, gift = weight_grad(joint_in[s], split(grad_qkv[s]), core, dp)
        keep, gift, grad_qkv = tie(keep, gift, grad_qkv)
        last_rings.give(s, keep, gift)
    down_sum, grad_qkv = beat((down_sum, grad_qkv), last_rings)
    outputs, gate_two = [], []
    for s in range(2):
        out, total = stage(
            leave_kernel,
            live,
            [*down_sum[s], residual[s], cotangents[s], down_biases[s : s + 1], mod[s]],
            [rows_of[s], 1],
            [BF16, F32],
            "leave",
        )
        outputs.append(out)
        gate_two.append(total)
    qv_sums = []
    for s in range(2):
        total = jnp.sum(grad_qkv[s].astype(F32), axis=0).reshape(-1, 3, lanes)
        qv_sums += [total[:, 0], total[:, 2]]
    unit_sums = jnp.concatenate([u.reshape(-1) for u in qv_sums + up_sums])
    unit_size = unit_sums.size
    unit_sums = jnp.pad(unit_sums, (0, -unit_size % (seqs * width))).reshape(seqs, -1, width)
    unit_rows = unit_sums.shape[1]
    gate_two, unit_sums = beat((gate_two, unit_sums), last_rings)
    gate_two, unit_sums = beat((gate_two, unit_sums), rings)
    back, gate_two, unit_sums = tie(back, gate_two, unit_sums)

    input_grads, first_sums = [], []
    for s in range(2):
        grad, total = stage(
            enter_back_kernel,
            live,
            [*back[s], tokens[s], resid_grad[s], mod[s]],
            [rows_of[s], 2],
            [F32, F32],
            "enter_back",
        )
        input_grads.append(grad)
        first_sums.append(total)
    packed_sums, picks = [], []
    for s in range(2):
        at = len(packed_sums)
        packed_sums += [first_sums[s], middle_sums[s], gate_two[s]]
        picks += [(at, 0), (at, 1)] + [(at + 1, row) for row in range(3)] + [(at + 2, 0)]
    for array in proj_sums + branch_sum:
        picks.append((len(packed_sums), 0))
        packed_sums.append(array)
    token_rows = len(picks)
    picks += [(len(packed_sums), row) for row in range(unit_rows)]
    sums = pack(packed_sums + [unit_sums], picks, "pack")
    sums, input_grads = beat((sums, input_grads), last_rings)
    if mp == 2:
        other = lax.ppermute(sums, "mp", swap)
        row_of = lax.broadcasted_iota(jnp.int32, sums.shape, 1)
        other = jnp.where(row_of < token_rows, other.astype(F32), 0.0)
        sums = (sums.astype(F32) + other).astype(BF16)
    else:
        sums = jnp.concatenate(
            [lax.psum(sums[:, :token_rows], "mp"), sums[:, token_rows:]], axis=1
        )
    gathered = lax.all_gather(sums, "dp", axis=0, tiled=True)
    input_grads = beat(input_grads, last_rings)
    while rings.result is None:
        input_grads = beat(input_grads, rings)
    input_grads = beat(input_grads, last_rings)
    fc2_out, fc1_out = (jnp.stack([part[n] for part in rings.finish()]) for n in range(2))
    fc2_out = jnp.swapaxes(fc2_out, 1, 2)
    fc1_out, fc2_out = beat((fc1_out, fc2_out), last_rings)
    gathered, unused = tie(gathered, last_rings.sent)

    mod_all = [gathered[:, 6 * s : 6 * s + 6].reshape(dp * seqs, 6 * width) for s in range(2)]
    silu_grad = sum(dot(mod_all[s], ada_low[s], NT) for s in range(2))
    silu_grad = gather_small(silu_grad, lambda rows: beat(rows, last_rings))
    silu_grad, gathered = tie(silu_grad, gathered)
    silu_grad = lax.dynamic_slice_in_dim(silu_grad, my_dp * seqs, seqs, axis=1)
    silu_grad = jnp.moveaxis(silu_grad, 0, 1).reshape(seqs, -1)
    unused, pullback = jax.vjp(jax.nn.silu, condition.astype(F32))
    cond_out = pullback(silu_grad)[0]
    bias_all = jnp.sum(gathered[:, 12:token_rows].astype(F32), axis=0)
    unit_all = jnp.sum(gathered[:, token_rows:].astype(F32).reshape(dp, -1), axis=0)
    qv_size = qv_biases.size

    proj_out, qkv_out = (jnp.stack([part[n] for part in last_rings.finish()]) for n in range(2))
    proj_out = jnp.swapaxes(proj_out, 1, 2)
    qkv_out = qkv_out.reshape(2, share_rows, -1, 3, lanes)
    qkv_out = qkv_out.transpose(0, 3, 1, 2, 4).reshape(qkv_weight.shape)

    def own(total, axis):
        part = total.shape[axis] // dp
        return lax.dynamic_slice_in_dim(total, my_dp * part, part, axis=axis)

    proj_bias_out = own(bias_all[0:2], 1)
    fc2_bias_out = own(bias_all[2:4], 1)
    fc1_bias_out = own(unit_all[qv_size:unit_size].reshape(2, -1), 1)
    qv_bias_out = own(unit_all[:qv_size].reshape(qv_biases.shape), 2)
    ada_bias_out = own(jnp.stack([jnp.sum(m.astype(F32), axis=0) for m in mod_all]), 1)
    ada_out = jnp.stack([dot(silu_mine, mod_all[s], TN) for s in range(2)])

    return (
        outputs[0],
        outputs[1],
        ada_out,
        ada_bias_out,
        qkv_out,
        qv_bias_out,
        proj_out,
        proj_bias_out,
        fc1_out,
        fc1_bias_out,
        fc2_out,
        fc2_bias_out,
        input_grads[0],
        input_grads[1],
        cond_out,
    )


def solution(mesh):
    tokens = P("dp", "mp", None)
    weights = (
        P(None, ("mp", "dp"), None),
        P(None, "dp"),
        P(None, None, "dp", "mp"),
        P(None, None, ("mp", "dp")),
        P(None, "mp", "dp"),
        P(None, "dp"),
        P(None, "dp", "mp"),
        P(None, ("mp", "dp")),
        P(None, "mp", "dp"),
        P(None, "dp"),
    )
    return jax.shard_map(
        functools.partial(body, mesh.shape["mp"], mesh.shape["dp"]),
        mesh=mesh,
        in_specs=(tokens, tokens, P("dp", "mp"), P("dp", None)) + weights + (tokens, tokens),
        out_specs=(tokens, tokens) + weights + (tokens, tokens, P("dp", "mp")),
        check_vma=False,
    )
```
